128 devices in a mesh: gx: 8 (over z_lo, x), gy: 8 (over y, core), gz: 2 (over z_hi).
Axes of the slice: x: 4, y: 4, z: 4 (z_hi: 2, z_lo: 2; z = z_hi * 2 + z_lo), core: 2. Of those that a mesh axis runs over, the one named last changes fastest.
Arguments:
- sol_pos: float32 [3, 8, 8, 2, 49152], P(None, 'gx', 'gy', 'gz'), as said below
- sol_vel: float32 [3, 8, 8, 2, 49152], P(None, 'gx', 'gy', 'gz'), may hold values from -6 to 6
- sol_rows: int32 [8, 8, 2], P('gx', 'gy', 'gz'), may hold values from 192 to 384, as said below
- mig_pos: float32 [3, 8, 8, 2, 6, 3072], P(None, 'gx', 'gy', 'gz'), as said below
- mig_vel: float32 [3, 8, 8, 2, 6, 3072], P(None, 'gx', 'gy', 'gz'), may hold values from -6 to 6
- mig_rows: int32 [8, 8, 2, 6], P('gx', 'gy', 'gz'), may hold values from 0 to 24, as said below
- bead_pos: float32 [3, 8, 8, 2, 256], P(None, 'gx', 'gy', 'gz'), as said below
- bead_vel: float32 [3, 8, 8, 2, 256], P(None, 'gx', 'gy', 'gz'), may hold values from -2.7 to 2.7
- bead_chains: int32 [8, 8, 2], P('gx', 'gy', 'gz'), may hold values from 5 to 32, as said below
- bond_list: int32 [2, 8, 8, 2, 224], P(None, 'gx', 'gy', 'gz'), may hold values from 0 to 255, as said below
- cell_axis: int32 [128, 128, 64], P('gx', 'gy', 'gz'), may hold values from 0 to 31
- shift: int32 [3], replicated, may hold values from 0 to 15
Outputs:
- sol_pos_out: float32 [3, 8, 8, 2, 67584], P(None, 'gx', 'gy', 'gz')
- sol_vel_out: float32 [3, 8, 8, 2, 67584], P(None, 'gx', 'gy', 'gz')
- bead_pos_out: float32 [3, 8, 8, 2, 256], P(None, 'gx', 'gy', 'gz')
- bead_vel_out: float32 [3, 8, 8, 2, 256], P(None, 'gx', 'gy', 'gz')
The draws below stay inside these ranges and needn't reach their ends.
Inputs may be any that keep to these rules, and one draw needn't show every extreme that they name: `sol_rows`: some device's resident slots are all live. `mig_rows`: some device receives full buffers across all six faces. `sol_pos`: every resident position lies in its device's region (cells i * 16 to (i + 1) * 16 - 1 along the first dimension, likewise for the others), and x * 16 is at least 0.1 from a whole number. `mig_pos`: buffer f holds positions in the region of the neighbour across face f, with the same margin. `bead_pos`: beads lie in their device's region with the same margin; bonded live beads are 0.88 to 1.13 apart and no two live beads are closer than 0.88. `bead_chains`: some device holds 32 chains. `bond_list`: a live bond joins two live slots of its device.
All inputs are finite; a program needn't handle non-finite values.
Results may differ from the reference program's by a relative error of at most 0.0003.
Values sent between devices are 32-bit elements; how exact they have to be, the bound alone decides.
A program may use at most 128 MiB of HBM per device.

```python
import math
import jax
import jax.numpy as jnp
from jax import lax

CX = 16
CY = 16
CZ = 32
UNITS = 16
NAXES = 32
CHAIN = 8
CH_CAP = 32
M_ROWS = 24
NX = 128
NY = 128
NZ = 64
P_ROWS = 384
PCAP = 49152
MCAP = 3072
BEADS = 256
BONDS = 224
N_GX = 8
N_GY = 8
N_GZ = 2


def grid_counts():
    return (NX // CX, NY // CY, NZ // CZ)


def device_anchor(step_x, step_y, step_z):
    count_x, count_y, count_z = grid_counts()
    anchor_x = (jnp.arange(count_x) + step_x) % count_x * CX
    anchor_y = (jnp.arange(count_y) + step_y) % count_y * CY
    anchor_z = (jnp.arange(count_z) + step_z) % count_z * CZ
    return jnp.stack(jnp.broadcast_arrays(anchor_x[:, None, None], anchor_y[None, :, None], anchor_z[None, None, :])).astype(jnp.float32)


def fine_offset(key, extent_shape):
    return jax.random.uniform(key, extent_shape, jnp.float32, 0.1, 0.9)


def scatter_points(key, anchor, count):
    extent_shape = anchor.shape[1:] + (count,)
    streams = jax.random.split(key, 5)
    whole_cells = jnp.stack([jax.random.randint(streams[0], extent_shape, 0, CX), jax.random.randint(streams[1], extent_shape, 0, CY), jax.random.randint(streams[2], extent_shape, 0, CZ)])
    subcell = jax.random.randint(streams[3], (3,) + extent_shape, 0, UNITS)
    return anchor[..., None] + whole_cells.astype(jnp.float32) + (subcell.astype(jnp.float32) + fine_offset(streams[4], (3,) + extent_shape)) / UNITS


def draw_sol_pos(key, part):
    return scatter_points(jax.random.fold_in(key, 11), device_anchor(0, 0, 0), PCAP)


def draw_mig_pos(key, part):
    neighbours = [(-1, 0, 0), (1, 0, 0), (0, -1, 0), (0, 1, 0), (0, 0, -1), (0, 0, 1)]
    anchor = jnp.stack([device_anchor(offset_tuple[0], offset_tuple[1], offset_tuple[2]) for offset_tuple in neighbours], axis=-1)
    return scatter_points(jax.random.fold_in(key, 13), anchor, MCAP)


def draw_sol_rows(key, part):
    count_x, count_y, count_z = grid_counts()
    streams = jax.random.split(jax.random.fold_in(key, 17), 2)
    row_count = jax.random.randint(streams[0], (count_x * count_y * count_z,), P_ROWS // 2, P_ROWS + 1)
    chosen_dev = jax.random.randint(streams[1], (), 0, count_x * count_y * count_z)
    row_count = jnp.where(jnp.arange(count_x * count_y * count_z) == chosen_dev, P_ROWS, row_count)
    return row_count.reshape(count_x, count_y, count_z).astype(jnp.int32)


def draw_mig_rows(key, part):
    count_x, count_y, count_z = grid_counts()
    streams = jax.random.split(jax.random.fold_in(key, 19), 4)
    row_count = jax.random.randint(streams[0], (count_x, count_y, count_z, 6), 0, M_ROWS + 1)
    target_x = jax.random.randint(streams[1], (), 0, count_x)
    target_y = jax.random.randint(streams[2], (), 0, count_y)
    target_z = jax.random.randint(streams[3], (), 0, count_z)
    index_x = jnp.arange(count_x)[:, None, None, None]
    index_y = jnp.arange(count_y)[None, :, None, None]
    index_z = jnp.arange(count_z)[None, None, :, None]
    faces = jnp.arange(6)[None, None, None, :]
    face_dim = faces // 2
    face_sign = 2 * (faces % 2) - 1
    hit_x = (index_x + jnp.where(face_dim == 0, face_sign, 0)) % count_x == target_x
    hit_y = (index_y + jnp.where(face_dim == 1, face_sign, 0)) % count_y == target_y
    hit_z = (index_z + jnp.where(face_dim == 2, face_sign, 0)) % count_z == target_z
    full_face = hit_x & hit_y & hit_z
    return jnp.where(full_face, M_ROWS, row_count).astype(jnp.int32)


def fixed_segments():
    last_column = CX // CHAIN - 1
    plane = CY * CZ
    listed = [0, CZ - 1, (CY - 1) * CZ, last_column * plane + 4 * CZ + 4]
    if last_column > 0:
        listed.append(4 * CZ + 4)
    return listed


def bead_layout(key):
    count_x, count_y, count_z = grid_counts()
    devices = count_x * count_y * count_z
    streams = jax.random.split(jax.random.fold_in(key, 4242), 4)
    draw_level = jax.random.randint(streams[0], (devices,), 0, 16)
    chains = 5 + draw_level * draw_level * (CH_CAP - 5) // 225
    chosen_dev = jax.random.randint(streams[1], (), 0, devices)
    chains = jnp.where(jnp.arange(devices) == chosen_dev, CH_CAP, chains)
    segments = CX // CHAIN * CY * CZ
    fixed_rank = jnp.full((segments,), -1, jnp.int32)
    for rank_id, segment_id in enumerate(fixed_segments()):
        fixed_rank = fixed_rank.at[segment_id].set(rank_id)

    def pick_segments(sub_key):
        order = jax.random.permutation(sub_key, segments)
        place = jnp.argsort(order)
        score = jnp.where(fixed_rank >= 0, fixed_rank, 16 + place).astype(jnp.int32)
        return jnp.argsort(score)[:CH_CAP]
    chosen = jax.vmap(pick_segments)(jax.random.split(streams[2], devices))
    bead_ids = jnp.arange(BEADS)
    dead_flag = ((bead_ids // CHAIN)[None] >= chains[:, None]).astype(jnp.int32)
    scores = dead_flag * (4096 * BEADS) + jax.random.randint(streams[3], (devices, BEADS), 0, 4096) * BEADS + bead_ids[None]
    slot_bead = jnp.argsort(scores, axis=1)
    slot_of = jnp.argsort(slot_bead, axis=1)
    return (chains, chosen, slot_bead, slot_of)


def draw_bead_chains(key, part):
    count_x, count_y, count_z = grid_counts()
    chains, chosen, slot_bead, slot_of = bead_layout(key)
    return chains.reshape(count_x, count_y, count_z).astype(jnp.int32)


def draw_bond_list(key, part):
    count_x, count_y, count_z = grid_counts()
    chains, chosen, slot_bead, slot_of = bead_layout(key)
    bond_ids = jnp.arange(BONDS)
    head_bead = bond_ids // (CHAIN - 1) * CHAIN + bond_ids % (CHAIN - 1)
    first_end = slot_of[:, head_bead]
    second_end = slot_of[:, head_bead + 1]
    return jnp.stack([first_end, second_end]).reshape(2, count_x, count_y, count_z, BONDS).astype(jnp.int32)


def draw_bead_pos(key, part):
    count_x, count_y, count_z = grid_counts()
    devices = count_x * count_y * count_z
    chains, chosen, slot_bead, slot_of = bead_layout(key)
    chain_of = slot_bead // CHAIN
    place_in = slot_bead % CHAIN
    segment = jnp.take_along_axis(chosen, chain_of, axis=1)
    column = segment // (CY * CZ)
    remain = segment % (CY * CZ)
    lattice = jnp.stack([column * CHAIN + place_in, remain // CZ, remain % CZ]).astype(jnp.float32)
    anchor = device_anchor(0, 0, 0).reshape(3, devices, 1)
    streams = jax.random.split(jax.random.fold_in(key, 77), 2)
    subcell = jax.random.randint(streams[0], (3, devices, BEADS), 0, 2) + UNITS // 2 - 1
    placed = anchor + lattice + (subcell.astype(jnp.float32) + fine_offset(streams[1], (3, devices, BEADS))) / UNITS
    return placed.reshape(3, count_x, count_y, count_z, BEADS)


def plant(result, own_key, smallest, high):
    longest = result.shape.index(max(result.shape))
    spots = []
    for shift in (0, 1):
        where = [jax.random.randint(jax.random.fold_in(own_key, axis), (), 0, length) for axis, length in enumerate(result.shape)]
        where[longest] = (where[longest] + shift) % result.shape[longest]
        spots.append(tuple(where))
    return result.at[spots[0]].set(smallest).at[spots[1]].set(high)


def steps_of(rng, dims, cuts, least, high):
    def one(dim, blocks):
        heights = jax.random.uniform(jax.random.fold_in(jax.random.fold_in(rng, 6), dim), (blocks,), jnp.float32, least / len(cuts), high / len(cuts))
        return jnp.repeat(jnp.exp(heights), dims[dim] // blocks).reshape((-1,) + (1,) * (len(dims) - dim - 1))

    level = one(*cuts[0])
    for cut in cuts[1:]:
        level = level * one(*cut)
    return level


def normal_values(own_key, dims, width, bound, cuts=(), held_as=jnp.bfloat16):
    array = jax.random.normal(own_key, dims, jnp.float32) * width
    if len(cuts) > 0:
        array = steps_of(own_key, dims, cuts, -0.22, 0.18) * array
    return jnp.clip(array, min=-bound, max=bound).astype(held_as)


def setup_inputs(seed: int = 0) -> dict:
    streams_of = jax.random.split(jax.random.key(seed), 13)
    sol_pos = draw_sol_pos(jax.random.fold_in(streams_of[12], 71), 0)
    sol_vel = normal_values(streams_of[1], (3, N_GX, N_GY, N_GZ, PCAP), 1.0, 6.0, ((1, 8), (2, 8), (3, 2)), jnp.float32)
    sol_rows = draw_sol_rows(jax.random.fold_in(streams_of[12], 71), 0)
    mig_pos = draw_mig_pos(jax.random.fold_in(streams_of[12], 71), 0)
    mig_vel = normal_values(streams_of[4], (3, N_GX, N_GY, N_GZ, 6, MCAP), 1.0, 6.0, ((1, 8), (2, 8), (3, 2)), jnp.float32)
    mig_rows = draw_mig_rows(jax.random.fold_in(streams_of[12], 71), 0)
    bead_pos = draw_bead_pos(jax.random.fold_in(streams_of[12], 71), 0)
    bead_vel = normal_values(streams_of[7], (3, N_GX, N_GY, N_GZ, BEADS), 0.45, 2.7, ((1, 8), (2, 8), (3, 2)), jnp.float32)
    bead_chains = draw_bead_chains(jax.random.fold_in(streams_of[12], 71), 0)
    bond_list = draw_bond_list(jax.random.fold_in(streams_of[12], 71), 0)
    cell_axis = plant(jax.random.randint(streams_of[10], (NX, NY, NZ), 0, NAXES), jax.random.fold_in(streams_of[10], 1), 0, NAXES - 1).astype(jnp.int32)
    shift = jax.random.randint(streams_of[11], (3,), 0, UNITS).astype(jnp.int32)
    return dict(sol_pos=sol_pos, sol_vel=sol_vel, sol_rows=sol_rows, mig_pos=mig_pos, mig_vel=mig_vel, mig_rows=mig_rows, bead_pos=bead_pos, bead_vel=bead_vel, bead_chains=bead_chains, bond_list=bond_list, cell_axis=cell_axis, shift=shift)


bead_mass = 5.0
step_size = 0.02
spring = 30.0
reach_square = 2.25
far_point = -1000.0
cut_square = 2.0 ** (1.0 / 3.0)
turn_cosine = math.cos(130.0 * math.pi / 180.0)
turn_sine = math.sin(130.0 * math.pi / 180.0)
golden = math.pi * (3.0 - math.sqrt(5.0))

def axis_table():
    counter = jnp.arange(NAXES).astype(jnp.float32)
    height = 1.0 - (2.0 * counter + 1.0) / NAXES
    radius = jnp.sqrt(1.0 - height * height)
    return jnp.stack([radius * jnp.cos(golden * counter), radius * jnp.sin(golden * counter), height])

def rotate(relative, normal):
    along_axis = lax.optimization_barrier(jnp.sum(normal * relative, axis=0, keepdims=True))
    crossed = jnp.stack([normal[1] * relative[2] - normal[2] * relative[1], normal[2] * relative[0] - normal[0] * relative[2], normal[0] * relative[1] - normal[1] * relative[0]])
    return turn_cosine * relative + turn_sine * crossed + (1.0 - turn_cosine) * along_axis * normal

def pair_force(own_rows, ghost_rows):

    def add_block(running, ghost_block):
        differ = own_rows[:, :, None] - ghost_block[:, None, :]
        square = lax.optimization_barrier(jnp.sum(differ * differ, axis=0))
        inside = (square < cut_square) & (square > 0.25)
        inverse = 1.0 / jnp.where(inside, square, 1.0)
        sixth_power = inverse * inverse * inverse
        weight = jnp.where(inside, 24.0 * (2.0 * sixth_power * sixth_power - sixth_power) * inverse, 0.0)
        return (running + lax.optimization_barrier(jnp.sum(weight[None] * differ, axis=2)), None)
    running, unused = lax.scan(add_block, jnp.zeros_like(own_rows), ghost_rows)
    return running

def bond_force(own_rows, bond_pairs, bond_live):
    differ = own_rows[:, bond_pairs[0]] - own_rows[:, bond_pairs[1]]
    square = lax.optimization_barrier(jnp.sum(differ * differ, axis=0))
    weight = jnp.where(bond_live, -spring / (1.0 - square / reach_square), 0.0)
    pulling = weight[None] * differ
    slot_ids = jnp.arange(own_rows.shape[1], dtype=jnp.int32)
    first_hot = (bond_pairs[0][:, None] == slot_ids[None]).astype(own_rows.dtype)
    second_hot = (bond_pairs[1][:, None] == slot_ids[None]).astype(own_rows.dtype)
    return jnp.dot(pulling, first_hot, precision=lax.Precision.HIGHEST) - jnp.dot(pulling, second_hot, precision=lax.Precision.HIGHEST)

def ghost_blocks(position):
    count_x, count_y, count_z = position.shape[1:4]
    index_x = jnp.arange(count_x)[:, None, None]
    index_y = jnp.arange(count_y)[None, :, None]
    index_z = jnp.arange(count_z)[None, None, :]
    blocks = []
    for step_x in (-1, 0, 1):
        for step_y in (-1, 0, 1):
            for step_z in (-1, 0, 1):
                rolled = jnp.roll(position, (-step_x, -step_y, -step_z), axis=(1, 2, 3))
                image_shift = jnp.stack(jnp.broadcast_arrays(NX * ((index_x + step_x) // count_x), NY * ((index_y + step_y) // count_y), NZ * ((index_z + step_z) // count_z))).astype(position.dtype)
                blocks.append(rolled + image_shift[..., None])
    return jnp.stack(blocks, axis=4)

def all_forces(position, bond_pairs, bond_live):
    full_shape = position.shape
    devices = full_shape[1] * full_shape[2] * full_shape[3]
    ghosts = ghost_blocks(position).reshape(3, devices, 27, full_shape[4]).transpose(1, 2, 0, 3)
    own_all = position.reshape(3, devices, full_shape[4]).transpose(1, 0, 2)
    pair_all = bond_pairs.reshape(2, devices, -1).transpose(1, 0, 2)
    live_all = bond_live.reshape(devices, -1)

    def one_device(pieces):
        own_rows, ghost_rows, pair_rows, live_rows = pieces
        return pair_force(own_rows, ghost_rows) + bond_force(own_rows, pair_rows, live_rows)
    pushes = lax.map(one_device, (own_all, ghosts, pair_all, live_all))
    return pushes.transpose(1, 0, 2).reshape(full_shape)

def arrivals(buffers):
    pieces = []
    for face_id in range(6):
        along_axis = 1 + face_id // 2
        if face_id % 2 == 0:
            pieces.append(jnp.roll(buffers[:, :, :, :, face_id + 1], 1, axis=along_axis))
        else:
            pieces.append(jnp.roll(buffers[:, :, :, :, face_id - 1], -1, axis=along_axis))
    return jnp.concatenate(pieces, axis=-1)

def global_cell(position, shift):
    offset = shift.astype(position.dtype).reshape((3,) + (1,) * (position.ndim - 1))
    levels = jnp.floor(position * UNITS + offset).astype(jnp.int32) // UNITS
    return (levels[0] % NX * NY + levels[1] % NY) * NZ + levels[2] % NZ

def reference(sol_pos, sol_vel, sol_rows, mig_pos, mig_vel, mig_rows, bead_pos, bead_vel, bead_chains, bond_list, cell_axis, shift):
    resident_live = jnp.arange(PCAP, dtype=jnp.int32) < (128 * sol_rows)[..., None]
    arriving_rows = arrivals(mig_rows[None, ..., None])[0]
    arriving_live = jnp.arange(MCAP, dtype=jnp.int32) < (128 * arriving_rows)[..., None]
    arriving_live = arriving_live.reshape(arriving_live.shape[:3] + (6 * MCAP,))
    solvent_live = jnp.concatenate([resident_live, arriving_live], axis=-1)
    solvent_pos = jnp.concatenate([sol_pos, arrivals(mig_pos)], axis=-1)
    solvent_vel = jnp.concatenate([sol_vel, arrivals(mig_vel)], axis=-1)
    bead_live = jnp.arange(BEADS, dtype=jnp.int32) < (CHAIN * bead_chains)[..., None]
    bond_live = jnp.arange(BONDS, dtype=jnp.int32) < ((CHAIN - 1) * bead_chains)[..., None]
    solvent_count = solvent_live.size
    position = jnp.concatenate([solvent_pos.reshape(3, -1), bead_pos.reshape(3, -1)], axis=1)
    velocity = jnp.concatenate([solvent_vel.reshape(3, -1), bead_vel.reshape(3, -1)], axis=1)
    weight = jnp.concatenate([solvent_live.reshape(-1).astype(jnp.float32), bead_mass * bead_live.reshape(-1).astype(jnp.float32)])
    cell_id = global_cell(position, shift)
    moments = jnp.concatenate([weight[None], weight[None] * velocity], axis=0)
    moment_sums = jax.ops.segment_sum(moments.T, cell_id, num_segments=NX * NY * NZ)
    cell_mean = moment_sums[:, 1:] / jnp.maximum(moment_sums[:, :1], 1.0)
    normals = axis_table()[:, cell_axis.reshape(-1)]
    local_flow = cell_mean[cell_id].T
    collided = local_flow + rotate(velocity - local_flow, normals[:, cell_id])
    sol_new = collided[:, :solvent_count].reshape(solvent_vel.shape)
    bead_new = collided[:, solvent_count:].reshape(bead_vel.shape)
    sol_vel_out = jnp.where(solvent_live[None], sol_new, 0.0)
    cell_offset = solvent_pos - jnp.floor(solvent_pos) - 0.5
    sol_pos_out = jnp.where(solvent_live[None], cell_offset + 3.0 * step_size * sol_new, 0.0)
    half_kick = 0.5 * step_size / bead_mass

    def masked(bead_at):
        return jnp.where(bead_live[None], bead_at, far_point)
    moved = jnp.zeros_like(bead_pos)
    bead_speed = bead_new
    pushes = all_forces(masked(bead_pos + moved), bond_list, bond_live)
    for substep in range(3):
        bead_speed = bead_speed + half_kick * pushes
        moved = moved + step_size * bead_speed
        pushes = all_forces(masked(bead_pos + moved), bond_list, bond_live)
        bead_speed = bead_speed + half_kick * pushes
    return (sol_pos_out, sol_vel_out, jnp.where(bead_live[None], moved, 0.0), jnp.where(bead_live[None], bead_speed, 0.0))
```

```python
import math

import jax
import jax.numpy as jnp
import numpy as np
from jax import lax
from jax.experimental import pallas as pl
from jax.experimental.pallas import tpu as pltpu
from jax.sharding import PartitionSpec as P

BF = jnp.bfloat16
F32 = jnp.float32
MESH = pl.DeviceIdType.MESH

UNITS = 16
NAXES = 32
CHAIN = 8
bead_mass = 5.0
step_size = 0.02
spring = 30.0
reach_square = 2.25
far_point = -1000.0
cut_square = 2.0 ** (1.0 / 3.0)
turn_cosine = math.cos(130.0 * math.pi / 180.0)
turn_sine = math.sin(130.0 * math.pi / 180.0)
golden = math.pi * (3.0 - math.sqrt(5.0))

LANES = 256
LEVELS = 38
CH = 8
TROWS = LEVELS * CH
RES = 384
FACE = 24
SOLV = RES + 6 * FACE
ALL = SOLV + 8
KR = 24
BEADS = 256
BONDS = 224

OFFSETS = [
    (dx, dy, dz)
    for dx in (-1, 0, 1)
    for dy in (-1, 0, 1)
    for dz in (0, 1)
    if (dx, dy, dz) != (0, 0, 0)
]
HALO = [(1, 0, 0), (0, 1, 0), (0, 0, 1), (1, 0, 1), (0, 1, 1), (1, 1, 0), (1, 1, 1)]


def slot(dx, dy, dz):
    return ((dx + 1) * 3 + dy + 1) * 2 + dz


def axis_rows():
    counter = np.arange(128) % NAXES
    height = 1.0 - (2.0 * counter + 1.0) / NAXES
    radius = np.sqrt(1.0 - height * height)
    rows = np.stack(
        [radius * np.cos(golden * counter), radius * np.sin(golden * counter), height]
    )
    return np.repeat(rows, 8, axis=0).astype(np.float32)


def split2(value):
    high = value.astype(BF).astype(F32)
    return high, (value - high).astype(BF).astype(F32)


def split3(value):
    high = value.astype(BF)
    rest = value - high.astype(F32)
    middle = rest.astype(BF)
    low = (rest - middle.astype(F32)).astype(BF)
    return high, middle, low


def nt(a, b):
    return lax.dot_general(a, b, (((1,), (1,)), ((), ())), preferred_element_type=F32)


def nn(a, b):
    return lax.dot_general(a, b, (((1,), (0,)), ((), ())), preferred_element_type=F32)


def rows_of(ref, row, count):
    return jnp.broadcast_to(ref[pl.ds(row, 1), :], (count, 128))


def rotated(v, u, n):
    w = [v[d] - u[d] for d in range(3)]
    along = (1.0 - turn_cosine) * (n[0] * w[0] + n[1] * w[1] + n[2] * w[2])
    crossed = [
        n[1] * w[2] - n[2] * w[1],
        n[2] * w[0] - n[0] * w[2],
        n[0] * w[1] - n[1] * w[0],
    ]
    return [u[d] + turn_cosine * w[d] + turn_sine * crossed[d] + along * n[d] for d in range(3)]


def kernel(
    sol_rows,
    mig_rows,
    chains,
    shift,
    sol_pos,
    sol_vel,
    mig_pos,
    mig_vel,
    bead_pos,
    bead_vel,
    bond_list,
    cell_axis,
    axis_tab,
    pos_out,
    vel_out,
    bpos_out,
    bvel_out,
    lo_s,
    hi_s,
    V_s,
    acc,
    iota_lo,
    iota_hi,
    arr_pos,
    arr_vel,
    arr_rows,
    row_send,
    bpack,
    mom,
    E_s,
    D_s,
    sx,
    sy,
    sz,
    se,
    rx,
    ry,
    rz,
    re,
    ux,
    uy,
    uz,
    ue,
    gx_,
    gy_,
    gz_,
    ge,
    U_s,
    T_f,
    T_s,
    psend,
    ghost,
    G_s,
    GT_s,
    F_s,
    W_s,
    mig_ss,
    mig_rs,
    halo_ss,
    halo_rs,
    info_ss,
    info_rs,
    bead_ss,
    bead_rs,
):
    ix = lax.axis_index("gx")
    iy = lax.axis_index("gy")
    iz = lax.axis_index("gz")

    def device(dx, dy, dz):
        return (
            lax.rem(ix + dx + 8, 8),
            lax.rem(iy + dy + 8, 8),
            lax.rem(iz + dz + 2, 2),
        )

    barrier = pltpu.get_barrier_semaphore()
    for off in OFFSETS:
        pl.semaphore_signal(barrier, inc=1, device_id=device(*off), device_id_type=MESH)

    iota_lo[...] = lax.broadcasted_iota(jnp.int32, (256, 128), 0).astype(F32).astype(BF)
    iota_hi[...] = (
        (lax.broadcasted_iota(jnp.int32, (TROWS, 128), 0) // CH).astype(F32).astype(BF)
    )
    acc[...] = jnp.zeros_like(acc)
    bpack[...] = jnp.zeros_like(bpack)
    one16 = jnp.ones((16, 128), BF)
    zero16 = jnp.zeros((16, 128), BF)
    sub8 = lax.broadcasted_iota(jnp.int32, (8, 128), 0)
    lane256 = lax.broadcasted_iota(jnp.int32, (1, 256), 1)
    anchor = [(ix * 16).astype(F32), (iy * 16).astype(F32), (iz * 32).astype(F32)]
    shifts = [shift[d].astype(F32) for d in range(3)]
    bead_live = lane256 < CHAIN * chains[0]
    bond_live = lane256 < (CHAIN - 1) * chains[0]

    start = [bead_pos[d] for d in range(3)]

    def place(exchange, value):
        for d in range(3):
            psend[exchange, d : d + 1, :] = jnp.where(bead_live, value[d], far_point)
        psend[exchange, 3:4, :] = jnp.zeros((1, 256), F32)

    place(0, start)
    for g in range(6):
        row_send[g] = jnp.broadcast_to(mig_rows[g], (1, 128)).astype(jnp.int32)

    def prep(row0, p, v, weight):
        level = []
        for d in range(3):
            level.append(jnp.floor((p[d] * 16.0 + shifts[d]) * 0.0625) - anchor[d])
        lx, ly, lz = level
        xe = lx > 15.5
        ye = ly > 15.5
        ze = lz > 31.5
        zb = jnp.where(lz > 15.5, 1.0, 0.0)
        zm = lz - 16.0 * zb
        both = xe & ye
        edge = xe | ye
        along = jnp.where(xe, ly, lx)
        lo_edge = jnp.where(
            both,
            32.0 + lz,
            jnp.where(ze, along + jnp.where(xe, 0.0, 16.0), along * 16.0 + zm),
        )
        hi_edge = jnp.where(both | ze, 37.0, jnp.where(xe, 33.0, 35.0) + zb)
        lo_s[pl.ds(row0, 8), :] = jnp.where(edge, lo_edge, lx * 16.0 + ly)
        hi_s[pl.ds(row0, 8), :] = jnp.where(edge, hi_edge, lz)
        V_s[pl.ds(row0 * 8, 8, stride=8), :] = weight
        for d in range(3):
            high, low = split2(weight * v[d])
            V_s[pl.ds(row0 * 8 + 1 + d, 8, stride=8), :] = high
            V_s[pl.ds(row0 * 8 + 4 + d, 8, stride=8), :] = low
        V_s[pl.ds(row0 * 8 + 7, 8, stride=8), :] = jnp.zeros((8, 128), F32)

    def resident_prep(b, carry):
        r = pl.multiple_of(b * 8, 8)
        weight = jnp.where(sub8 + r < sol_rows[0], 1.0, 0.0)
        prep(
            r,
            [sol_pos[d, pl.ds(r, 8), :] for d in range(3)],
            [sol_vel[d, pl.ds(r, 8), :] for d in range(3)],
            weight,
        )
        return carry

    lax.fori_loop(0, RES // 8, resident_prep, 0)

    row32 = lax.broadcasted_iota(jnp.int32, (32, 256), 0)
    col32 = lax.broadcasted_iota(jnp.int32, (32, 256), 1)
    mask_face = (col32 % 16) == (row32 % 16)
    mask_edge = (
        ((col32 < 32) & (row32 == 0))
        | ((col32 >= 32) & (col32 < 64) & (col32 - 32 == row32))
        | ((col32 == 64) & (row32 == 0))
    )
    er = lax.broadcasted_iota(jnp.int32, (256, 256), 0)
    ec = lax.broadcasted_iota(jnp.int32, (256, 256), 1)

    def as_bf(mask):
        return jnp.where(mask, 1.0, 0.0).astype(BF)

    E_s[0:256, :] = as_bf(ec == er // 16)
    E_s[256:512, :] = as_bf(ec == (er // 16) * 16)
    target = jnp.where(er < 16, er, jnp.where(er < 32, (er - 16) * 16, 0))
    E_s[512:768, :] = as_bf(ec == target)
    first = jnp.where(bond_live, bond_list[0], -1)
    second = jnp.where(bond_live, bond_list[1], -1)
    D_s[...] = (
        jnp.where(er == first, 1.0, 0.0) - jnp.where(er == second, 1.0, 0.0)
    ).astype(BF)

    pl.semaphore_wait(barrier, len(OFFSETS))

    faces = [(-1, 0, 0), (1, 0, 0), (0, -1, 0), (0, 1, 0), (0, 0, 1), (0, 0, 1)]

    def mig_copies(g, f):
        where = dict(device_id=device(*faces[g]), device_id_type=MESH)
        return [
            pltpu.make_async_remote_copy(
                src_ref=mig_pos.at[:, g],
                dst_ref=arr_pos.at[:, f],
                send_sem=mig_ss.at[0, g],
                recv_sem=mig_rs.at[0, f],
                **where,
            ),
            pltpu.make_async_remote_copy(
                src_ref=mig_vel.at[:, g],
                dst_ref=arr_vel.at[:, f],
                send_sem=mig_ss.at[1, g],
                recv_sem=mig_rs.at[1, f],
                **where,
            ),
            pltpu.make_async_remote_copy(
                src_ref=row_send.at[g],
                dst_ref=arr_rows.at[f],
                send_sem=mig_ss.at[2, g],
                recv_sem=mig_rs.at[2, f],
                **where,
            ),
        ]

    def bead_copy(exchange, off, into):
        return pltpu.make_async_remote_copy(
            src_ref=psend.at[exchange],
            dst_ref=ghost.at[exchange, into],
            send_sem=bead_ss.at[exchange, slot(*off)],
            recv_sem=bead_rs.at[exchange, into],
            device_id=device(*off),
            device_id_type=MESH,
        )

    def bead_send(exchange):
        for dx, dy, dz in OFFSETS:
            bead_copy(exchange, (dx, dy, dz), slot(-dx, -dy, dz)).start()

    def bead_arrive(exchange):
        for off in OFFSETS:
            bead_copy(exchange, off, slot(*off)).wait_recv()

    bead_send(0)
    for g in range(6):
        for copy in mig_copies(g, g ^ 1):
            copy.start()

    def hot_lo(row):
        lo_b = rows_of(lo_s, row, 16).astype(BF)
        return jnp.concatenate(
            [
                jnp.where(iota_lo[16 * j : 16 * j + 16, :] == lo_b, one16, zero16)
                for j in range(16)
            ],
            0,
        )

    def bin_rows(row0, count):
        spread = []
        hot = []
        for r in range(count):
            row = row0 + r
            hot.append(hot_lo(row))
            v = V_s[pl.ds(pl.multiple_of(row * 8, 8), 8), :]
            v = jnp.concatenate([v, v], 0).astype(BF)
            hi_b = rows_of(hi_s, row, 16).astype(BF)
            spread.append(
                jnp.concatenate(
                    [
                        jnp.where(iota_hi[16 * j : 16 * j + 16, :] == hi_b, v, zero16)
                        for j in range(TROWS // 16)
                    ],
                    0,
                )
            )
        sums = nt(jnp.concatenate(spread, 1), jnp.concatenate(hot, 1))
        acc[0:TROWS, :] += sums[:, 0:128]
        acc[TROWS : 2 * TROWS, :] += sums[:, 128:256]

    def bin_loop(b, carry):
        bin_rows(b * KR, KR)
        return carry

    lax.fori_loop(0, RES // KR, bin_loop, 0)

    for f in range(6):
        for copy in mig_copies(f, f):
            copy.wait_recv()

    def arrival_prep(f, carry):
        for b in range(FACE // 8):
            live = (sub8 + 8 * b) < arr_rows[f]
            prep(
                pl.multiple_of(RES + f * FACE + 8 * b, 8),
                [arr_pos[d, f, 8 * b : 8 * b + 8, :] for d in range(3)],
                [arr_vel[d, f, 8 * b : 8 * b + 8, :] for d in range(3)],
                jnp.where(live, 1.0, 0.0),
            )
        return carry

    lax.fori_loop(0, 6, arrival_prep, 0)
    for d in range(3):
        for h in range(2):
            half = slice(128 * h, 128 * h + 128)
            bpack[d, h : h + 1, :] = start[d][:, half]
            bpack[3 + d, h : h + 1, :] = bead_vel[d][:, half]
    lane8 = lax.broadcasted_iota(jnp.int32, (8, 128), 1) + 128 * sub8
    bead_here = (lane8 < CHAIN * chains[0]) & (sub8 < 2)
    prep(
        SOLV,
        [bpack[d] for d in range(3)],
        [bpack[3 + d] for d in range(3)],
        jnp.where(bead_here, bead_mass, 0.0),
    )
    lax.fori_loop(RES // KR, SOLV // KR, bin_loop, 0)
    bin_rows(SOLV, 2)

    for c in range(4):
        for h in range(2):
            value = acc[pl.ds(h * TROWS + c, LEVELS, stride=8), :]
            if c > 0:
                value += acc[pl.ds(h * TROWS + c + 3, LEVELS, stride=8), :]
            mom[c, 0:LEVELS, 128 * h : 128 * h + 128] = value
    for c in range(4):
        sz[c : c + 1, :] = mom[c, 32:33, :]
        sx[2 * c : 2 * c + 2, :] = mom[c, 33:35, :]
        sy[2 * c : 2 * c + 2, :] = mom[c, 35:37, :]
        se[c : c + 1, :] = mom[c, 37:38, :]

    def halo_copies(src, dst, ss, rs, sign):
        copies = []
        for i, (dx, dy, dz) in enumerate(HALO):
            s = src[min(i, 3)]
            t = dst[i] if i < 3 else dst[3].at[i - 3]
            copies.append(
                pltpu.make_async_remote_copy(
                    src_ref=s,
                    dst_ref=t,
                    send_sem=ss.at[i],
                    recv_sem=rs.at[i],
                    device_id=device(sign * dx, sign * dy, dz),
                    device_id_type=MESH,
                )
            )
        return copies

    halo = halo_copies((sx, sy, sz, se), (rx, ry, rz, re), halo_ss, halo_rs, 1)
    for copy in halo:
        copy.start()

    row_c = lax.broadcasted_iota(jnp.int32, (1, 128), 1)
    block = row_c // 4
    comp = row_c % 4
    bx = block // 6 - 1
    by = (block // 2) % 3 - 1
    wrap_x = jnp.where(ix + bx < 0, -128.0, jnp.where(ix + bx > 7, 128.0, 0.0))
    wrap_y = jnp.where(iy + by < 0, -128.0, jnp.where(iy + by > 7, 128.0, 0.0))
    image = jnp.where(comp == 0, wrap_x, jnp.where(comp == 1, wrap_y, 0.0))
    wrapped = (comp == 2) & (block % 2 == 1)
    centre = anchor[2] + 16.0
    G_s[...] = jnp.zeros_like(G_s)

    def forces(exchange):
        own = slot(0, 0, 0)
        for k in range(18):
            if k == own:
                G_s[4 * k : 4 * k + 4, :] = psend[exchange]
            else:
                G_s[4 * k : 4 * k + 4, :] = ghost[exchange, k]
        GT = G_s[...].T + image
        turns = jnp.floor((GT - centre) * (1.0 / 64.0) + 0.5)
        GT_s[...] = jnp.where(wrapped, GT - 64.0 * turns, GT)
        here = [
            [
                jnp.broadcast_to(psend[exchange, d : d + 1, 128 * h : 128 * h + 128], (8, 128))
                for d in range(3)
            ]
            for h in range(2)
        ]

        def group(j, sums):
            tile = GT_s[pl.ds(pl.multiple_of(8 * j, 8), 8), :]
            sums = list(sums)
            for k in range(18):
                other = [
                    jnp.broadcast_to(tile[:, 4 * k + d : 4 * k + d + 1], (8, 128))
                    for d in range(3)
                ]
                for h in range(2):
                    differ = [here[h][d] - other[d] for d in range(3)]
                    square = (
                        differ[0] * differ[0] + differ[1] * differ[1] + differ[2] * differ[2]
                    )
                    inside = (square < cut_square) & (square > 0.25)
                    inverse = 1.0 / jnp.where(inside, square, 1.0)
                    sixth = inverse * inverse * inverse
                    weight = jnp.where(inside, (48.0 * sixth - 24.0) * sixth * inverse, 0.0)
                    for d in range(3):
                        sums[3 * h + d] = sums[3 * h + d] + weight * differ[d]
            return tuple(sums)

        zero = jnp.zeros((8, 128), F32)
        sums = lax.fori_loop(0, 32, group, (zero,) * 6)
        for h in range(2):
            for d in range(3):
                F_s[d : d + 1, 128 * h : 128 * h + 128] = jnp.sum(
                    sums[3 * h + d], axis=0, keepdims=True
                )
        pieces = split3(jnp.concatenate([psend[exchange], psend[exchange]], 0))
        hot = D_s[...]
        differ = nn(pieces[0], hot) + nn(pieces[1], hot) + nn(pieces[2], hot)
        square = jnp.sum(jnp.where(sub256 < 3, differ * differ, 0.0), axis=0, keepdims=True)
        weight = jnp.where(bond_live, -spring / (1.0 - square / reach_square), 0.0)
        pieces = split3(weight * differ)
        pull = nt(pieces[0], hot) + nt(pieces[1], hot) + nt(pieces[2], hot)
        return [F_s[d : d + 1, :] + pull[d : d + 1, :] for d in range(3)]

    sub256 = lax.broadcasted_iota(jnp.int32, (8, 256), 0)
    F_s[...] = jnp.zeros_like(F_s)
    bead_arrive(0)
    push = forces(0)

    for copy in halo_copies((sx, sy, sz, se), (rx, ry, rz, re), halo_ss, halo_rs, -1):
        copy.wait_recv()
    zero_face = jnp.zeros((32, 256), F32)
    spread = []
    for c in range(4):
        edge = jnp.where(
            lane256 < 16,
            re[0, c : c + 1, :],
            jnp.where(
                lane256 < 32,
                re[1, c : c + 1, :],
                jnp.where(lane256 < 64, re[2, c : c + 1, :], re[3, c : c + 1, :]),
            ),
        )
        low_half = row32 < 16
        vx = jnp.where(low_half, rx[2 * c : 2 * c + 1, :], rx[2 * c + 1 : 2 * c + 2, :])
        vy = jnp.where(low_half, ry[2 * c : 2 * c + 1, :], ry[2 * c + 1 : 2 * c + 2, :])
        spread.append(
            jnp.concatenate(
                [
                    jnp.where(mask_face, vx, zero_face),
                    jnp.where(mask_face, vy, zero_face),
                    jnp.where(mask_edge, edge, zero_face),
                ],
                1,
            )
        )
    pieces = split3(jnp.concatenate(spread, 0))
    moved = nn(pieces[0], E_s[...]) + nn(pieces[1], E_s[...]) + nn(pieces[2], E_s[...])
    total = []
    for c in range(4):
        value = mom[c, 0:32, :] + moved[32 * c : 32 * c + 32, :]
        total.append(value + jnp.where(row32 == 0, rz[c : c + 1, :], 0.0))
    scale = 1.0 / jnp.maximum(total[0], 1.0)
    eye = (
        lax.broadcasted_iota(jnp.int32, (32, 32), 0) == lax.broadcasted_iota(jnp.int32, (32, 32), 1)
    )
    axis_here = nt(as_bf(eye), cell_axis[...].astype(F32).astype(BF))
    parts = [None] * 8
    for d in range(3):
        parts[d], parts[3 + d] = split2(total[1 + d] * scale)
    parts[6] = axis_here
    parts[7] = zero_face
    for c in range(8):
        for h in range(2):
            T_f[pl.ds(h * TROWS + c, 32, stride=8), :] = parts[c][:, 128 * h : 128 * h + 128]
    picked = nt(jnp.concatenate(parts[:7], 0).astype(BF), E_s[...])
    for q in range(4):
        if q < 3:
            value = picked[32 * q : 32 * q + 32, :] + picked[96 + 32 * q : 128 + 32 * q, :]
            uz[q : q + 1, :] = parts[q][0:1, :] + parts[3 + q][0:1, :]
        else:
            value = picked[192:224, :]
            uz[q : q + 1, :] = parts[6][0:1, :]
        vx = jnp.where(mask_face, value[:, 0:256], 0.0)
        vy = jnp.where(mask_face, value[:, 256:512], 0.0)
        ve = jnp.where(mask_edge, value[:, 512:768], 0.0)
        for j in range(2):
            half = slice(16 * j, 16 * j + 16)
            ux[2 * q + j : 2 * q + j + 1, :] = jnp.sum(vx[half], axis=0, keepdims=True)
            uy[2 * q + j : 2 * q + j + 1, :] = jnp.sum(vy[half], axis=0, keepdims=True)
        ue[q : q + 1, :] = jnp.sum(ve, axis=0, keepdims=True)
    info = halo_copies((ux, uy, uz, ue), (gx_, gy_, gz_, ge), info_ss, info_rs, -1)
    for copy in info:
        copy.start()
    for copy in halo_copies((ux, uy, uz, ue), (gx_, gy_, gz_, ge), info_ss, info_rs, 1):
        copy.wait_recv()

    def halo_level(level, channel, value):
        for h in range(2):
            row = h * TROWS + 8 * level + channel
            T_f[row : row + 1, :] = value[:, 128 * h : 128 * h + 128]

    for q in range(4):
        edge = jnp.where(
            lane256 < 16,
            ge[0, q : q + 1, :],
            jnp.where(
                lane256 < 32,
                ge[1, q : q + 1, :],
                jnp.where(lane256 < 64, ge[2, q : q + 1, :], ge[3, q : q + 1, :]),
            ),
        )
        edge = jnp.where(lane256 < 65, edge, 0.0)
        values = [gz_[q : q + 1, :]]
        values += [gx_[2 * q + j : 2 * q + j + 1, :] for j in range(2)]
        values += [gy_[2 * q + j : 2 * q + j + 1, :] for j in range(2)]
        values += [edge]
        for i, value in enumerate(values):
            if q < 3:
                high, low = split2(value)
                halo_level(32 + i, q, high)
                halo_level(32 + i, 3 + q, low)
            else:
                halo_level(32 + i, 6, value)
                halo_level(32 + i, 7, jnp.zeros((1, 256), F32))
    for h in range(2):
        half = slice(128 * h, 128 * h + 128)
        T_s[:, half] = T_f[h * TROWS : h * TROWS + TROWS, :].astype(BF)

    def look_rows(row0, count):
        hot = jnp.concatenate([hot_lo(row0 + r) for r in range(count)], 1)
        found = nn(T_s[...], hot)
        for r in range(count):
            row = row0 + r
            level = rows_of(hi_s, row, 8).astype(jnp.int32)
            values = [
                found[8 * j : 8 * j + 8, 128 * r : 128 * r + 128] for j in range(LEVELS)
            ]
            bit = 1
            while len(values) > 1:
                odd = (level & bit) != 0
                values = [
                    jnp.where(odd, values[i + 1], values[i]) if i + 1 < len(values) else values[i]
                    for i in range(0, len(values), 2)
                ]
                bit = 2 * bit
            V_s[pl.ds(pl.multiple_of(row * 8, 8), 8), :] = values[0]

    def collide(row0, v):
        read = [V_s[pl.ds(row0 * 8 + c, 8, stride=8), :] for c in range(7)]
        u = [read[d] + read[3 + d] for d in range(3)]
        index = read[6].astype(jnp.int32)
        n = [
            jnp.take_along_axis(axis_tab[8 * d : 8 * d + 8, :], index, axis=1) for d in range(3)
        ]
        return rotated(v, u, n)

    def emit(row0, p, v, live):
        new = collide(row0, v)
        for d in range(3):
            offset = p[d] - jnp.floor(p[d]) - 0.5
            vel_out[d, pl.ds(row0, 8), :] = jnp.where(live, new[d], 0.0)
            pos_out[d, pl.ds(row0, 8), :] = jnp.where(
                live, offset + 3.0 * step_size * new[d], 0.0
            )

    def look_resident(b, carry):
        look_rows(b * KR, KR)
        for i in range(KR // 8):
            r = pl.multiple_of(b * KR + 8 * i, 8)
            emit(
                r,
                [sol_pos[d, pl.ds(r, 8), :] for d in range(3)],
                [sol_vel[d, pl.ds(r, 8), :] for d in range(3)],
                sub8 + r < sol_rows[0],
            )
        return carry

    def look_arrival(f, carry):
        look_rows(RES + f * FACE, FACE)
        for i in range(FACE // 8):
            emit(
                pl.multiple_of(RES + f * FACE + 8 * i, 8),
                [arr_pos[d, f, 8 * i : 8 * i + 8, :] for d in range(3)],
                [arr_vel[d, f, 8 * i : 8 * i + 8, :] for d in range(3)],
                (sub8 + 8 * i) < arr_rows[f],
            )
        return carry

    look_rows(SOLV, 2)
    new = collide(SOLV, [bpack[3 + d] for d in range(3)])
    speed = []
    for d in range(3):
        W_s[d] = new[d]
        speed.append(jnp.concatenate([W_s[d, 0:1, :], W_s[d, 1:2, :]], 1))

    half_kick = 0.5 * step_size / bead_mass
    gone = [jnp.zeros((1, 256), F32)] * 3
    for substep in range(3):
        speed = [speed[d] + half_kick * push[d] for d in range(3)]
        gone = [gone[d] + step_size * speed[d] for d in range(3)]
        place(substep + 1, [start[d] + gone[d] for d in range(3)])
        bead_send(substep + 1)
        if substep == 0:
            lax.fori_loop(0, 6, look_arrival, 0)
        else:
            lax.fori_loop(8 * (substep - 1), 8 * substep, look_resident, 0)
        bead_arrive(substep + 1)
        push = forces(substep + 1)
        speed = [speed[d] + half_kick * push[d] for d in range(3)]
    for d in range(3):
        bpos_out[d] = jnp.where(bead_live, gone[d], 0.0)
        bvel_out[d] = jnp.where(bead_live, speed[d], 0.0)

    for g in range(6):
        for copy in mig_copies(g, g ^ 1):
            copy.wait_send()
    for copy in halo:
        copy.wait_send()
    for copy in info:
        copy.wait_send()
    for exchange in range(4):
        for dx, dy, dz in OFFSETS:
            bead_copy(exchange, (dx, dy, dz), slot(-dx, -dy, dz)).wait_send()


def shards(
    sol_pos,
    sol_vel,
    sol_rows,
    mig_pos,
    mig_vel,
    mig_rows,
    bead_pos,
    bead_vel,
    bead_chains,
    bond_list,
    cell_axis,
    shift,
):
    vmem = pl.BlockSpec(memory_space=pltpu.VMEM)
    smem = pl.BlockSpec(memory_space=pltpu.SMEM)
    bonds = jnp.pad(bond_list.reshape(2, 1, BONDS), ((0, 0), (0, 0), (0, 256 - BONDS)))
    dma = pltpu.SemaphoreType.DMA
    f32 = lambda *shape: pltpu.VMEM(shape, F32)
    bf = lambda *shape: pltpu.VMEM(shape, BF)
    outs = pl.pallas_call(
        kernel,
        out_shape=(
            jax.ShapeDtypeStruct((3, SOLV, 128), F32),
            jax.ShapeDtypeStruct((3, SOLV, 128), F32),
            jax.ShapeDtypeStruct((3, 1, BEADS), F32),
            jax.ShapeDtypeStruct((3, 1, BEADS), F32),
        ),
        in_specs=[smem] * 4 + [vmem] * 9,
        out_specs=(vmem,) * 4,
        scratch_shapes=[
            f32(ALL, 128),
            f32(ALL, 128),
            f32(ALL * 8, 128),
            f32(2 * TROWS, 128),
            bf(256, 128),
            bf(TROWS, 128),
            f32(3, 6, FACE, 128),
            f32(3, 6, FACE, 128),
            pltpu.VMEM((6, 1, 128), jnp.int32),
            pltpu.VMEM((6, 1, 128), jnp.int32),
            f32(6, 8, 128),
            f32(4, 40, 256),
            bf(768, 256),
            bf(256, 256),
            f32(8, 256),
            f32(8, 256),
            f32(4, 256),
            f32(4, 256),
            f32(8, 256),
            f32(8, 256),
            f32(4, 256),
            f32(4, 4, 256),
            f32(8, 256),
            f32(8, 256),
            f32(4, 256),
            f32(4, 256),
            f32(8, 256),
            f32(8, 256),
            f32(4, 256),
            f32(4, 4, 256),
            f32(4, 32, 256),
            f32(2 * TROWS, 128),
            bf(TROWS, 256),
            f32(4, 4, 256),
            f32(4, 18, 4, 256),
            f32(128, 256),
            f32(256, 128),
            f32(8, 256),
            f32(3, 8, 128),
            dma((3, 6)),
            dma((3, 6)),
            dma((7,)),
            dma((7,)),
            dma((7,)),
            dma((7,)),
            dma((4, 18)),
            dma((4, 18)),
        ],
        compiler_params=pltpu.CompilerParams(
            collective_id=0, has_side_effects=True, vmem_limit_bytes=60 * 1024 * 1024
        ),
        name="interval",
    )(
        sol_rows.reshape(1),
        mig_rows.reshape(6),
        bead_chains.reshape(1),
        shift,
        sol_pos.reshape(3, RES, 128),
        sol_vel.reshape(3, RES, 128),
        mig_pos.reshape(3, 6, FACE, 128),
        mig_vel.reshape(3, 6, FACE, 128),
        bead_pos.reshape(3, 1, BEADS),
        bead_vel.reshape(3, 1, BEADS),
        bonds,
        cell_axis.reshape(256, 32),
        jnp.asarray(axis_rows()),
    )
    pos, vel, bpos, bvel = outs
    return (
        pos.reshape(3, 1, 1, 1, SOLV * 128),
        vel.reshape(3, 1, 1, 1, SOLV * 128),
        bpos.reshape(3, 1, 1, 1, BEADS),
        bvel.reshape(3, 1, 1, 1, BEADS),
    )


def solution(mesh):
    return jax.shard_map(
        shards,
        mesh=mesh,
        in_specs=(
            P(None, "gx", "gy", "gz", None),
            P(None, "gx", "gy", "gz", None),
            P("gx", "gy", "gz"),
            P(None, "gx", "gy", "gz", None, None),
            P(None, "gx", "gy", "gz", None, None),
            P("gx", "gy", "gz", None),
            P(None, "gx", "gy", "gz", None),
            P(None, "gx", "gy", "gz", None),
            P("gx", "gy", "gz"),
            P(None, "gx", "gy", "gz", None),
            P("gx", "gy", "gz"),
            P(),
        ),
        out_specs=(
            P(None, "gx", "gy", "gz", None),
            P(None, "gx", "gy", "gz", None),
            P(None, "gx", "gy", "gz", None),
            P(None, "gx", "gy", "gz", None),
        ),
        check_vma=False,
    )
```

```python
import math

import jax
import jax.numpy as jnp
import numpy as np
from jax import lax
from jax.experimental import pallas as pl
from jax.experimental.pallas import tpu as pltpu
from jax.sharding import PartitionSpec as P

BF = jnp.bfloat16
F32 = jnp.float32
MESH = pl.DeviceIdType.MESH

UNITS = 16
NAXES = 32
CHAIN = 8
bead_mass = 5.0
step_size = 0.02
spring = 30.0
reach_square = 2.25
far_point = -1000.0
cut_square = 2.0 ** (1.0 / 3.0)
turn_cosine = math.cos(130.0 * math.pi / 180.0)
turn_sine = math.sin(130.0 * math.pi / 180.0)
golden = math.pi * (3.0 - math.sqrt(5.0))

LANES = 256
LEVELS = 38
CH = 8
TROWS = LEVELS * CH
RES = 384
FACE = 24
SOLV = RES + 6 * FACE
ALL = SOLV + 8
KR = 24
BEADS = 256
BONDS = 224

OFFSETS = [
    (dx, dy, dz)
    for dx in (-1, 0, 1)
    for dy in (-1, 0, 1)
    for dz in (0, 1)
    if (dx, dy, dz) != (0, 0, 0)
]
HALO = [(1, 0, 0), (0, 1, 0), (0, 0, 1), (1, 0, 1), (0, 1, 1), (1, 1, 0), (1, 1, 1)]


def slot(dx, dy, dz):
    return ((dx + 1) * 3 + dy + 1) * 2 + dz


def axis_rows():
    counter = np.arange(128) % NAXES
    height = 1.0 - (2.0 * counter + 1.0) / NAXES
    radius = np.sqrt(1.0 - height * height)
    rows = np.stack(
        [radius * np.cos(golden * counter), radius * np.sin(golden * counter), height]
    )
    return np.repeat(rows, 8, axis=0).astype(np.float32)


def split2(value):
    high = value.astype(BF).astype(F32)
    return high, (value - high).astype(BF).astype(F32)


def split3(value):
    high = value.astype(BF)
    rest = value - high.astype(F32)
    middle = rest.astype(BF)
    low = (rest - middle.astype(F32)).astype(BF)
    return high, middle, low


def nt(a, b):
    return lax.dot_general(a, b, (((1,), (1,)), ((), ())), preferred_element_type=F32)


def nn(a, b):
    return lax.dot_general(a, b, (((1,), (0,)), ((), ())), preferred_element_type=F32)


def rows_of(ref, row, count):
    return jnp.broadcast_to(ref[pl.ds(row, 1), :], (count, 128))


def rotated(v, u, n):
    w = [v[d] - u[d] for d in range(3)]
    along = (1.0 - turn_cosine) * (n[0] * w[0] + n[1] * w[1] + n[2] * w[2])
    crossed = [
        n[1] * w[2] - n[2] * w[1],
        n[2] * w[0] - n[0] * w[2],
        n[0] * w[1] - n[1] * w[0],
    ]
    return [u[d] + turn_cosine * w[d] + turn_sine * crossed[d] + along * n[d] for d in range(3)]


def kernel(
    sol_rows,
    mig_rows,
    chains,
    shift,
    sol_pos_hbm,
    sol_vel_hbm,
    mig_pos,
    mig_vel,
    bead_pos,
    bead_vel,
    bond_list,
    cell_axis,
    axis_tab,
    off_hbm,
    vel_hbm,
    bpos_out,
    bvel_out,
    sol_pos,
    sol_vel,
    off_out,
    vel_out,
    bond_s,
    lo_s,
    hi_s,
    V_s,
    acc,
    iota_lo,
    iota_hi,
    arr_pos,
    arr_vel,
    arr_rows,
    row_send,
    bpack,
    mom,
    E_s,
    D_s,
    sx,
    sy,
    sz,
    se,
    rx,
    ry,
    rz,
    re,
    ux,
    uy,
    uz,
    ue,
    gx_,
    gy_,
    gz_,
    ge,
    U_s,
    T_f,
    T_s,
    psend,
    ghost,
    G_s,
    GT_s,
    P_s,
    M_s,
    A_s,
    W_s,
    mig_ss,
    mig_rs,
    halo_ss,
    halo_rs,
    info_ss,
    info_rs,
    bead_ss,
    bead_rs,
    in_sem,
    out_sem,
):
    ix = lax.axis_index("gx")
    iy = lax.axis_index("gy")
    iz = lax.axis_index("gz")

    def device(dx, dy, dz):
        return (
            lax.rem(ix + dx + 8, 8),
            lax.rem(iy + dy + 8, 8),
            lax.rem(iz + dz + 2, 2),
        )

    barrier = pltpu.get_barrier_semaphore()
    for off in OFFSETS:
        pl.semaphore_signal(barrier, inc=1, device_id=device(*off), device_id_type=MESH)

    HALF = RES // 2

    def in_copies(chunk):
        part = pl.ds(chunk * HALF, HALF)
        return [
            pltpu.make_async_copy(
                sol_pos_hbm.at[:, part], sol_pos.at[:, part], in_sem.at[0, chunk]
            ),
            pltpu.make_async_copy(
                sol_vel_hbm.at[:, part], sol_vel.at[:, part], in_sem.at[1, chunk]
            ),
        ]

    for chunk in range(2):
        for copy in in_copies(chunk):
            copy.start()

    iota_lo[...] = lax.broadcasted_iota(jnp.int32, (256, 128), 0).astype(F32).astype(BF)
    iota_hi[...] = (
        (lax.broadcasted_iota(jnp.int32, (TROWS, 128), 0) // CH).astype(F32).astype(BF)
    )
    acc[...] = jnp.zeros_like(acc)
    bpack[...] = jnp.zeros_like(bpack)
    one16 = jnp.ones((16, 128), BF)
    zero16 = jnp.zeros((16, 128), BF)
    sub8 = lax.broadcasted_iota(jnp.int32, (8, 128), 0)
    lane256 = lax.broadcasted_iota(jnp.int32, (1, 256), 1)
    anchor = [(ix * 16).astype(F32), (iy * 16).astype(F32), (iz * 32).astype(F32)]
    shifts = [shift[d].astype(F32) for d in range(3)]
    bead_live = lane256 < CHAIN * chains[0]
    bond_live = lane256 < (CHAIN - 1) * chains[0]

    start = [bead_pos[d] for d in range(3)]

    def place(exchange, value):
        for d in range(3):
            psend[exchange, d : d + 1, :] = jnp.where(bead_live, value[d], far_point)
        psend[exchange, 3:4, :] = jnp.zeros((1, 256), F32)

    place(0, start)
    for g in range(6):
        row_send[g] = jnp.broadcast_to(mig_rows[g], (1, 128)).astype(jnp.int32)

    def prep(row0, p, v, weight):
        level = []
        for d in range(3):
            level.append(jnp.floor((p[d] * 16.0 + shifts[d]) * 0.0625) - anchor[d])
        lx, ly, lz = level
        xe = lx > 15.5
        ye = ly > 15.5
        ze = lz > 31.5
        zb = jnp.where(lz > 15.5, 1.0, 0.0)
        zm = lz - 16.0 * zb
        both = xe & ye
        edge = xe | ye
        along = jnp.where(xe, ly, lx)
        lo_edge = jnp.where(
            both,
            32.0 + lz,
            jnp.where(ze, along + jnp.where(xe, 0.0, 16.0), along * 16.0 + zm),
        )
        hi_edge = jnp.where(both | ze, 37.0, jnp.where(xe, 33.0, 35.0) + zb)
        lo_s[pl.ds(row0, 8), :] = jnp.where(edge, lo_edge, lx * 16.0 + ly)
        hi_s[pl.ds(row0, 8), :] = jnp.where(edge, hi_edge, lz)
        V_s[pl.ds(row0 * 8, 8, stride=8), :] = weight
        for d in range(3):
            high, low = split2(weight * v[d])
            V_s[pl.ds(row0 * 8 + 1 + d, 8, stride=8), :] = high
            V_s[pl.ds(row0 * 8 + 4 + d, 8, stride=8), :] = low
        V_s[pl.ds(row0 * 8 + 7, 8, stride=8), :] = jnp.zeros((8, 128), F32)

    def resident_prep(b, carry):
        r = pl.multiple_of(b * 8, 8)
        weight = jnp.where(sub8 + r < sol_rows[0], 1.0, 0.0)
        prep(
            r,
            [sol_pos[d, pl.ds(r, 8), :] for d in range(3)],
            [sol_vel[d, pl.ds(r, 8), :] for d in range(3)],
            weight,
        )
        return carry

    faces = [(-1, 0, 0), (1, 0, 0), (0, -1, 0), (0, 1, 0), (0, 0, 1), (0, 0, 1)]

    def mig_copies(g, f):
        where = dict(device_id=device(*faces[g]), device_id_type=MESH)
        return [
            pltpu.make_async_remote_copy(
                src_ref=mig_pos.at[:, g],
                dst_ref=arr_pos.at[:, f],
                send_sem=mig_ss.at[0, g],
                recv_sem=mig_rs.at[0, f],
                **where,
            ),
            pltpu.make_async_remote_copy(
                src_ref=mig_vel.at[:, g],
                dst_ref=arr_vel.at[:, f],
                send_sem=mig_ss.at[1, g],
                recv_sem=mig_rs.at[1, f],
                **where,
            ),
            pltpu.make_async_remote_copy(
                src_ref=row_send.at[g],
                dst_ref=arr_rows.at[f],
                send_sem=mig_ss.at[2, g],
                recv_sem=mig_rs.at[2, f],
                **where,
            ),
        ]

    def bead_copy(exchange, off, into):
        return pltpu.make_async_remote_copy(
            src_ref=psend.at[exchange],
            dst_ref=ghost.at[exchange, into],
            send_sem=bead_ss.at[exchange, slot(*off)],
            recv_sem=bead_rs.at[exchange, into],
            device_id=device(*off),
            device_id_type=MESH,
        )

    def bead_send(exchange):
        for dx, dy, dz in OFFSETS:
            bead_copy(exchange, (dx, dy, dz), slot(-dx, -dy, dz)).start()

    def bead_arrive(exchange):
        for off in OFFSETS:
            bead_copy(exchange, off, slot(*off)).wait_recv()

    def hot_lo(row):
        lo_b = rows_of(lo_s, row, 16).astype(BF)
        return jnp.concatenate(
            [
                jnp.where(iota_lo[16 * j : 16 * j + 16, :] == lo_b, one16, zero16)
                for j in range(16)
            ],
            0,
        )

    def bin_rows(row0, count):
        spread = []
        hot = []
        for r in range(count):
            row = row0 + r
            hot.append(hot_lo(row))
            v = V_s[pl.ds(pl.multiple_of(row * 8, 8), 8), :]
            v = jnp.concatenate([v, v], 0).astype(BF)
            hi_b = rows_of(hi_s, row, 16).astype(BF)
            spread.append(
                jnp.concatenate(
                    [
                        jnp.where(iota_hi[16 * j : 16 * j + 16, :] == hi_b, v, zero16)
                        for j in range(TROWS // 16)
                    ],
                    0,
                )
            )
        sums = nt(jnp.concatenate(spread, 1), jnp.concatenate(hot, 1))
        acc[0:TROWS, :] += sums[:, 0:128]
        acc[TROWS : 2 * TROWS, :] += sums[:, 128:256]

    def bin_loop(b, carry):
        bin_rows(b * KR, KR)
        return carry

    for copy in in_copies(0):
        copy.wait()
    lax.fori_loop(0, HALF // 8, resident_prep, 0)
    lax.fori_loop(0, HALF // KR, bin_loop, 0)
    for copy in in_copies(1):
        copy.wait()
    lax.fori_loop(HALF // 8, RES // 8, resident_prep, 0)

    pl.semaphore_wait(barrier, len(OFFSETS))
    bead_send(0)
    for g in range(6):
        for copy in mig_copies(g, g ^ 1):
            copy.start()

    lax.fori_loop(HALF // KR, RES // KR, bin_loop, 0)

    for f in range(6):
        for copy in mig_copies(f, f):
            copy.wait_recv()

    def arrival_prep(f, carry):
        for b in range(FACE // 8):
            live = (sub8 + 8 * b) < arr_rows[f]
            prep(
                pl.multiple_of(RES + f * FACE + 8 * b, 8),
                [arr_pos[d, f, 8 * b : 8 * b + 8, :] for d in range(3)],
                [arr_vel[d, f, 8 * b : 8 * b + 8, :] for d in range(3)],
                jnp.where(live, 1.0, 0.0),
            )
        return carry

    lax.fori_loop(0, 6, arrival_prep, 0)
    for d in range(3):
        for h in range(2):
            half = slice(128 * h, 128 * h + 128)
            bpack[d, h : h + 1, :] = start[d][:, half]
            bpack[3 + d, h : h + 1, :] = bead_vel[d][:, half]
    lane8 = lax.broadcasted_iota(jnp.int32, (8, 128), 1) + 128 * sub8
    bead_here = (lane8 < CHAIN * chains[0]) & (sub8 < 2)
    prep(
        SOLV,
        [bpack[d] for d in range(3)],
        [bpack[3 + d] for d in range(3)],
        jnp.where(bead_here, bead_mass, 0.0),
    )
    lax.fori_loop(RES // KR, SOLV // KR, bin_loop, 0)
    bin_rows(SOLV, 2)

    for c in range(4):
        for h in range(2):
            value = acc[pl.ds(h * TROWS + c, LEVELS, stride=8), :]
            if c > 0:
                value += acc[pl.ds(h * TROWS + c + 3, LEVELS, stride=8), :]
            mom[c, 0:LEVELS, 128 * h : 128 * h + 128] = value
    for c in range(4):
        sz[c : c + 1, :] = mom[c, 32:33, :]
        sx[2 * c : 2 * c + 2, :] = mom[c, 33:35, :]
        sy[2 * c : 2 * c + 2, :] = mom[c, 35:37, :]
        se[c : c + 1, :] = mom[c, 37:38, :]

    def halo_copies(src, dst, ss, rs, sign):
        copies = []
        for i, (dx, dy, dz) in enumerate(HALO):
            s = src[min(i, 3)]
            t = dst[i] if i < 3 else dst[3].at[i - 3]
            copies.append(
                pltpu.make_async_remote_copy(
                    src_ref=s,
                    dst_ref=t,
                    send_sem=ss.at[i],
                    recv_sem=rs.at[i],
                    device_id=device(sign * dx, sign * dy, dz),
                    device_id_type=MESH,
                )
            )
        return copies

    halo = halo_copies((sx, sy, sz, se), (rx, ry, rz, re), halo_ss, halo_rs, 1)
    for copy in halo:
        copy.start()

    row32 = lax.broadcasted_iota(jnp.int32, (32, 256), 0)
    col32 = lax.broadcasted_iota(jnp.int32, (32, 256), 1)
    mask_face = (col32 % 16) == (row32 % 16)
    mask_edge = (
        ((col32 < 32) & (row32 == 0))
        | ((col32 >= 32) & (col32 < 64) & (col32 - 32 == row32))
        | ((col32 == 64) & (row32 == 0))
    )
    er = lax.broadcasted_iota(jnp.int32, (256, 256), 0)
    ec = lax.broadcasted_iota(jnp.int32, (256, 256), 1)

    def as_bf(mask):
        return jnp.where(mask, 1.0, 0.0).astype(BF)

    E_s[0:256, :] = as_bf(ec == er // 16)
    E_s[256:512, :] = as_bf(ec == (er // 16) * 16)
    target = jnp.where(er < 16, er, jnp.where(er < 32, (er - 16) * 16, 0))
    E_s[512:768, :] = as_bf(ec == target)
    bond_s[:, :, 0:BONDS] = bond_list[...]
    first = jnp.where(bond_live, bond_s[0], -1)
    second = jnp.where(bond_live, bond_s[1], -1)
    D_s[...] = (
        jnp.where(er == first, 1.0, 0.0) - jnp.where(er == second, 1.0, 0.0)
    ).astype(BF)

    row_c = lax.broadcasted_iota(jnp.int32, (72, 256), 0)
    block = row_c // 4
    comp = row_c % 4
    bx = block // 6 - 1
    by = (block // 2) % 3 - 1
    wrap_x = jnp.where(ix + bx < 0, -128.0, jnp.where(ix + bx > 7, 128.0, 0.0))
    wrap_y = jnp.where(iy + by < 0, -128.0, jnp.where(iy + by > 7, 128.0, 0.0))
    image = jnp.where(comp == 0, wrap_x, jnp.where(comp == 1, wrap_y, 0.0))
    wrapped = (comp == 2) & (block % 2 == 1)
    centre = anchor[2] + 16.0
    upper = ((comp == 0) & (bx == 1)) | ((comp == 1) & (by == 1))
    G_s[...] = jnp.zeros_like(G_s)

    def forces(exchange):
        own = slot(0, 0, 0)
        for k in range(18):
            if k == own:
                G_s[0:4, :] = psend[exchange]
                P_s[4 * k : 4 * k + 4, :] = psend[exchange]
            else:
                P_s[4 * k : 4 * k + 4, :] = ghost[exchange, k]
        GT_s[...] = G_s[...].T
        at = P_s[...] + image
        turns = jnp.floor((at - centre) * (1.0 / 64.0) + 0.5)
        at = jnp.where(wrapped, at - 64.0 * turns, at)
        at = jnp.where(upper & (at < -500.0), -3.0 * far_point, at)
        P_s[...] = at
        M_s[0:24, :] = 0.5 * (at[0:24] + at[48:72])
        M_s[24:32, :] = 0.5 * (at[24:32] + at[40:48])

        def group(j, carry):
            here = []
            for t in range(2):
                tile = GT_s[pl.ds(pl.multiple_of(16 * j + 8 * t, 8), 8), :]
                here.append([jnp.broadcast_to(tile[:, d : d + 1], (8, 128)) for d in range(3)])
            twice = [here[t][1] + here[t][1] for t in range(2)]
            sums = [jnp.zeros((8, 128), F32) for i in range(6)]

            def choose(mask, a, b):
                return [jnp.where(mask, a[d], b[d]) for d in range(3)]

            def add(t, other):
                differ = [here[t][d] - other[d] for d in range(3)]
                square = differ[0] * differ[0] + differ[1] * differ[1] + differ[2] * differ[2]
                inverse = 1.0 / jnp.where(square > 0.25, square, 1.0e6)
                sixth = inverse * inverse * inverse
                weight = jnp.maximum(48.0 * sixth - 24.0, 0.0) * sixth * inverse
                for d in range(3):
                    sums[3 * t + d] = sums[3 * t + d] + weight * differ[d]

            for h in range(2):
                half = slice(128 * h, 128 * h + 128)

                def row(ref, r):
                    return jnp.broadcast_to(ref[r : r + 1, half], (8, 128))

                def ghost_at(dx, dy, dz):
                    return [row(P_s, 4 * slot(dx, dy, dz) + d) for d in range(3)]

                for dz in (0, 1):
                    inner = ghost_at(0, 0, dz)
                    for t in range(2):
                        add(t, inner)
                    low, high = ghost_at(0, -1, dz), ghost_at(0, 1, dz)
                    half_way = row(M_s, 4 * slot(0, -1, dz) + 1)
                    for t in range(2):
                        add(t, choose(here[t][1] < half_way, low, high))
                    near = [[], []]
                    for dy in (0, -1, 1):
                        low, high = ghost_at(-1, dy, dz), ghost_at(1, dy, dz)
                        half_way = row(M_s, 4 * slot(-1, dy, dz))
                        for t in range(2):
                            near[t].append(choose(here[t][0] < half_way, low, high))
                    for t in range(2):
                        side, low, high = near[t]
                        add(t, side)
                        add(t, choose(twice[t] < low[1] + high[1], low, high))
            for t in range(2):
                for d in range(3):
                    A_s[pl.ds(pl.multiple_of(256 * d + 16 * j + 8 * t, 8), 8), :] = sums[3 * t + d]
            return carry

        lax.fori_loop(0, 16, group, 0)
        ones = jnp.ones((8, 128), BF)
        pieces = split3(A_s[...])
        pair = nt(ones, pieces[0]) + nt(ones, pieces[1]) + nt(ones, pieces[2])
        pieces = split3(jnp.concatenate([psend[exchange], psend[exchange]], 0))
        hot = D_s[...]
        differ = nn(pieces[0], hot) + nn(pieces[1], hot) + nn(pieces[2], hot)
        square = jnp.sum(jnp.where(sub256 < 3, differ * differ, 0.0), axis=0, keepdims=True)
        weight = jnp.where(bond_live, -spring / (1.0 - square / reach_square), 0.0)
        pieces = split3(weight * differ)
        pull = nt(pieces[0], hot) + nt(pieces[1], hot) + nt(pieces[2], hot)
        return [pair[0:1, 256 * d : 256 * d + 256] + pull[d : d + 1, :] for d in range(3)]

    sub256 = lax.broadcasted_iota(jnp.int32, (8, 256), 0)
    bead_arrive(0)
    push = forces(0)

    for copy in halo_copies((sx, sy, sz, se), (rx, ry, rz, re), halo_ss, halo_rs, -1):
        copy.wait_recv()
    zero_face = jnp.zeros((32, 256), F32)
    spread = []
    for c in range(4):
        edge = jnp.where(
            lane256 < 16,
            re[0, c : c + 1, :],
            jnp.where(
                lane256 < 32,
                re[1, c : c + 1, :],
                jnp.where(lane256 < 64, re[2, c : c + 1, :], re[3, c : c + 1, :]),
            ),
        )
        low_half = row32 < 16
        vx = jnp.where(low_half, rx[2 * c : 2 * c + 1, :], rx[2 * c + 1 : 2 * c + 2, :])
        vy = jnp.where(low_half, ry[2 * c : 2 * c + 1, :], ry[2 * c + 1 : 2 * c + 2, :])
        spread.append(
            jnp.concatenate(
                [
                    jnp.where(mask_face, vx, zero_face),
                    jnp.where(mask_face, vy, zero_face),
                    jnp.where(mask_edge, edge, zero_face),
                ],
                1,
            )
        )
    pieces = split3(jnp.concatenate(spread, 0))
    moved = nn(pieces[0], E_s[...]) + nn(pieces[1], E_s[...]) + nn(pieces[2], E_s[...])
    total = []
    for c in range(4):
        value = mom[c, 0:32, :] + moved[32 * c : 32 * c + 32, :]
        total.append(value + jnp.where(row32 == 0, rz[c : c + 1, :], 0.0))
    scale = 1.0 / jnp.maximum(total[0], 1.0)
    eye = (
        lax.broadcasted_iota(jnp.int32, (32, 32), 0) == lax.broadcasted_iota(jnp.int32, (32, 32), 1)
    )
    axis_here = nt(as_bf(eye), cell_axis[...].astype(F32).astype(BF))
    parts = [None] * 8
    for d in range(3):
        parts[d], parts[3 + d] = split2(total[1 + d] * scale)
    parts[6] = axis_here
    parts[7] = zero_face
    for c in range(8):
        for h in range(2):
            T_f[pl.ds(h * TROWS + c, 32, stride=8), :] = parts[c][:, 128 * h : 128 * h + 128]
    picked = nt(jnp.concatenate(parts[:7], 0).astype(BF), E_s[...])
    for q in range(4):
        if q < 3:
            value = picked[32 * q : 32 * q + 32, :] + picked[96 + 32 * q : 128 + 32 * q, :]
            uz[q : q + 1, :] = parts[q][0:1, :] + parts[3 + q][0:1, :]
        else:
            value = picked[192:224, :]
            uz[q : q + 1, :] = parts[6][0:1, :]
        vx = jnp.where(mask_face, value[:, 0:256], 0.0)
        vy = jnp.where(mask_face, value[:, 256:512], 0.0)
        ve = jnp.where(mask_edge, value[:, 512:768], 0.0)
        for j in range(2):
            half = slice(16 * j, 16 * j + 16)
            ux[2 * q + j : 2 * q + j + 1, :] = jnp.sum(vx[half], axis=0, keepdims=True)
            uy[2 * q + j : 2 * q + j + 1, :] = jnp.sum(vy[half], axis=0, keepdims=True)
        ue[q : q + 1, :] = jnp.sum(ve, axis=0, keepdims=True)
    info = halo_copies((ux, uy, uz, ue), (gx_, gy_, gz_, ge), info_ss, info_rs, -1)
    for copy in info:
        copy.start()
    for copy in halo_copies((ux, uy, uz, ue), (gx_, gy_, gz_, ge), info_ss, info_rs, 1):
        copy.wait_recv()

    def halo_level(level, channel, value):
        for h in range(2):
            row = h * TROWS + 8 * level + channel
            T_f[row : row + 1, :] = value[:, 128 * h : 128 * h + 128]

    for q in range(4):
        edge = jnp.where(
            lane256 < 16,
            ge[0, q : q + 1, :],
            jnp.where(
                lane256 < 32,
                ge[1, q : q + 1, :],
                jnp.where(lane256 < 64, ge[2, q : q + 1, :], ge[3, q : q + 1, :]),
            ),
        )
        edge = jnp.where(lane256 < 65, edge, 0.0)
        values = [gz_[q : q + 1, :]]
        values += [gx_[2 * q + j : 2 * q + j + 1, :] for j in range(2)]
        values += [gy_[2 * q + j : 2 * q + j + 1, :] for j in range(2)]
        values += [edge]
        for i, value in enumerate(values):
            if q < 3:
                high, low = split2(value)
                halo_level(32 + i, q, high)
                halo_level(32 + i, 3 + q, low)
            else:
                halo_level(32 + i, 6, value)
                halo_level(32 + i, 7, jnp.zeros((1, 256), F32))
    for h in range(2):
        half = slice(128 * h, 128 * h + 128)
        T_s[:, half] = T_f[h * TROWS : h * TROWS + TROWS, :].astype(BF)

    def look_rows(row0, count):
        hot = jnp.concatenate([hot_lo(row0 + r) for r in range(count)], 1)
        found = nn(T_s[...], hot)
        for r in range(count):
            row = row0 + r
            level = rows_of(hi_s, row, 8).astype(jnp.int32)
            values = [
                found[8 * j : 8 * j + 8, 128 * r : 128 * r + 128] for j in range(LEVELS)
            ]
            bit = 1
            while len(values) > 1:
                odd = (level & bit) != 0
                values = [
                    jnp.where(odd, values[i + 1], values[i]) if i + 1 < len(values) else values[i]
                    for i in range(0, len(values), 2)
                ]
                bit = 2 * bit
            V_s[pl.ds(pl.multiple_of(row * 8, 8), 8), :] = values[0]

    def collide(row0, v):
        read = [V_s[pl.ds(row0 * 8 + c, 8, stride=8), :] for c in range(7)]
        u = [read[d] + read[3 + d] for d in range(3)]
        index = read[6].astype(jnp.int32)
        n = [
            jnp.take_along_axis(axis_tab[8 * d : 8 * d + 8, :], index, axis=1) for d in range(3)
        ]
        return rotated(v, u, n)

    def emit(row0, p, v, live):
        new = collide(row0, v)
        for d in range(3):
            offset = p[d] - jnp.floor(p[d]) - 0.5
            vel_out[d, pl.ds(row0, 8), :] = new[d]
            off_out[d, pl.ds(row0, 8), :] = jnp.where(live, offset, 2.0)

    def look_resident(b, carry):
        look_rows(b * KR, KR)
        for i in range(KR // 8):
            r = pl.multiple_of(b * KR + 8 * i, 8)
            emit(
                r,
                [sol_pos[d, pl.ds(r, 8), :] for d in range(3)],
                [sol_vel[d, pl.ds(r, 8), :] for d in range(3)],
                sub8 + r < sol_rows[0],
            )
        return carry

    def look_arrival(f, carry):
        look_rows(RES + f * FACE, FACE)
        for i in range(FACE // 8):
            emit(
                pl.multiple_of(RES + f * FACE + 8 * i, 8),
                [arr_pos[d, f, 8 * i : 8 * i + 8, :] for d in range(3)],
                [arr_vel[d, f, 8 * i : 8 * i + 8, :] for d in range(3)],
                (sub8 + 8 * i) < arr_rows[f],
            )
        return carry

    look_rows(SOLV, 2)
    new = collide(SOLV, [bpack[3 + d] for d in range(3)])
    speed = []
    for d in range(3):
        W_s[d] = new[d]
        speed.append(jnp.concatenate([W_s[d, 0:1, :], W_s[d, 1:2, :]], 1))

    def out_copies(substep):
        part = pl.ds(RES, SOLV - RES) if substep == 0 else pl.ds((substep - 1) * HALF, HALF)
        return [
            pltpu.make_async_copy(
                off_out.at[:, part], off_hbm.at[:, part], out_sem.at[0, substep]
            ),
            pltpu.make_async_copy(
                vel_out.at[:, part], vel_hbm.at[:, part], out_sem.at[1, substep]
            ),
        ]

    half_kick = 0.5 * step_size / bead_mass
    gone = [jnp.zeros((1, 256), F32)] * 3
    for substep in range(3):
        speed = [speed[d] + half_kick * push[d] for d in range(3)]
        gone = [gone[d] + step_size * speed[d] for d in range(3)]
        place(substep + 1, [start[d] + gone[d] for d in range(3)])
        bead_send(substep + 1)
        if substep == 0:
            lax.fori_loop(0, 6, look_arrival, 0)
        else:
            lax.fori_loop(8 * (substep - 1), 8 * substep, look_resident, 0)
        for copy in out_copies(substep):
            copy.start()
        bead_arrive(substep + 1)
        push = forces(substep + 1)
        speed = [speed[d] + half_kick * push[d] for d in range(3)]
    for d in range(3):
        bpos_out[d] = gone[d]
        bvel_out[d] = speed[d]
    for substep in range(3):
        for copy in out_copies(substep):
            copy.wait()

    for g in range(6):
        for copy in mig_copies(g, g ^ 1):
            copy.wait_send()
    for copy in halo:
        copy.wait_send()
    for copy in info:
        copy.wait_send()
    for exchange in range(4):
        for dx, dy, dz in OFFSETS:
            bead_copy(exchange, (dx, dy, dz), slot(-dx, -dy, dz)).wait_send()


def shards(
    sol_pos,
    sol_vel,
    sol_rows,
    mig_pos,
    mig_vel,
    mig_rows,
    bead_pos,
    bead_vel,
    bead_chains,
    bond_list,
    cell_axis,
    shift,
):
    vmem = pl.BlockSpec(memory_space=pltpu.VMEM)
    smem = pl.BlockSpec(memory_space=pltpu.SMEM)
    anywhere = pl.BlockSpec(memory_space=pl.ANY)
    dma = pltpu.SemaphoreType.DMA
    f32 = lambda *shape: pltpu.VMEM(shape, F32)
    bf = lambda *shape: pltpu.VMEM(shape, BF)
    outs = pl.pallas_call(
        kernel,
        out_shape=(
            jax.ShapeDtypeStruct((3, SOLV, 128), F32),
            jax.ShapeDtypeStruct((3, SOLV, 128), F32),
            jax.ShapeDtypeStruct((3, 1, BEADS), F32),
            jax.ShapeDtypeStruct((3, 1, BEADS), F32),
        ),
        in_specs=[smem] * 4 + [anywhere] * 4 + [vmem] * 5,
        out_specs=(anywhere, anywhere, vmem, vmem),
        scratch_shapes=[
            f32(3, RES, 128),
            f32(3, RES, 128),
            f32(3, SOLV, 128),
            f32(3, SOLV, 128),
            pltpu.VMEM((2, 1, 256), jnp.int32),
            f32(ALL, 128),
            f32(ALL, 128),
            f32(ALL * 8, 128),
            f32(2 * TROWS, 128),
            bf(256, 128),
            bf(TROWS, 128),
            f32(3, 6, FACE, 128),
            f32(3, 6, FACE, 128),
            pltpu.VMEM((6, 1, 128), jnp.int32),
            pltpu.VMEM((6, 1, 128), jnp.int32),
            f32(6, 8, 128),
            f32(4, 40, 256),
            bf(768, 256),
            bf(256, 256),
            f32(8, 256),
            f32(8, 256),
            f32(4, 256),
            f32(4, 256),
            f32(8, 256),
            f32(8, 256),
            f32(4, 256),
            f32(4, 4, 256),
            f32(8, 256),
            f32(8, 256),
            f32(4, 256),
            f32(4, 256),
            f32(8, 256),
            f32(8, 256),
            f32(4, 256),
            f32(4, 4, 256),
            f32(4, 32, 256),
            f32(2 * TROWS, 128),
            bf(TROWS, 256),
            f32(4, 4, 256),
            f32(4, 18, 4, 256),
            f32(128, 256),
            f32(256, 128),
            f32(72, 256),
            f32(32, 256),
            f32(768, 128),
            f32(3, 8, 128),
            dma((3, 6)),
            dma((3, 6)),
            dma((7,)),
            dma((7,)),
            dma((7,)),
            dma((7,)),
            dma((4, 18)),
            dma((4, 18)),
            dma((2, 2)),
            dma((2, 3)),
        ],
        compiler_params=pltpu.CompilerParams(
            collective_id=0, has_side_effects=True, vmem_limit_bytes=60 * 1024 * 1024
        ),
        name="interval",
    )(
        sol_rows.reshape(1),
        mig_rows.reshape(6),
        bead_chains.reshape(1),
        shift,
        sol_pos.reshape(3, RES, 128),
        sol_vel.reshape(3, RES, 128),
        mig_pos.reshape(3, 6, FACE, 128),
        mig_vel.reshape(3, 6, FACE, 128),
        bead_pos.reshape(3, 1, BEADS),
        bead_vel.reshape(3, 1, BEADS),
        bond_list.reshape(2, 1, BONDS),
        cell_axis.reshape(256, 32),
        jnp.asarray(axis_rows()),
    )
    offset, vel, bpos, bvel = outs
    live = offset < 1.0
    bead_live = jnp.arange(BEADS, dtype=jnp.int32) < CHAIN * bead_chains.reshape(())
    return (
        jnp.where(live, offset + 3.0 * step_size * vel, 0.0).reshape(3, 1, 1, 1, SOLV * 128),
        jnp.where(live, vel, 0.0).reshape(3, 1, 1, 1, SOLV * 128),
        jnp.where(bead_live, bpos, 0.0).reshape(3, 1, 1, 1, BEADS),
        jnp.where(bead_live, bvel, 0.0).reshape(3, 1, 1, 1, BEADS),
    )


def solution(mesh):
    return jax.shard_map(
        shards,
        mesh=mesh,
        in_specs=(
            P(None, "gx", "gy", "gz", None),
            P(None, "gx", "gy", "gz", None),
            P("gx", "gy", "gz"),
            P(None, "gx", "gy", "gz", None, None),
            P(None, "gx", "gy", "gz", None, None),
            P("gx", "gy", "gz", None),
            P(None, "gx", "gy", "gz", None),
            P(None, "gx", "gy", "gz", None),
            P("gx", "gy", "gz"),
            P(None, "gx", "gy", "gz", None),
            P("gx", "gy", "gz"),
            P(),
        ),
        out_specs=(
            P(None, "gx", "gy", "gz", None),
            P(None, "gx", "gy", "gz", None),
            P(None, "gx", "gy", "gz", None),
            P(None, "gx", "gy", "gz", None),
        ),
        check_vma=False,
    )
```

```python
import math

import jax
import jax.numpy as jnp
import numpy as np
from jax import lax
from jax.experimental import pallas as pl
from jax.experimental.pallas import tpu as pltpu
from jax.sharding import PartitionSpec as P

BF = jnp.bfloat16
F32 = jnp.float32
MESH = pl.DeviceIdType.MESH

UNITS = 16
NAXES = 32
CHAIN = 8
bead_mass = 5.0
step_size = 0.02
spring = 30.0
reach_square = 2.25
far_point = -1000.0
cut_square = 2.0 ** (1.0 / 3.0)
turn_cosine = math.cos(130.0 * math.pi / 180.0)
turn_sine = math.sin(130.0 * math.pi / 180.0)
golden = math.pi * (3.0 - math.sqrt(5.0))

LANES = 256
LEVELS = 38
CH = 8
TROWS = LEVELS * CH
RES = 384
FACE = 24
SOLV = RES + 6 * FACE
ALL = SOLV + 8
STEP = 2 * FACE
BEADS = 256
BONDS = 224

OFFSETS = [
    (dx, dy, dz)
    for dx in (-1, 0, 1)
    for dy in (-1, 0, 1)
    for dz in (0, 1)
    if (dx, dy, dz) != (0, 0, 0)
]
FACES = [(-1, 0, 0), (1, 0, 0), (0, -1, 0), (0, 1, 0), (0, 0, 1)]
HALO = [(1, 0, 0), (0, 1, 0), (0, 0, 1), (1, 0, 1), (0, 1, 1), (1, 1, 0), (1, 1, 1)]


def slot(dx, dy, dz):
    return ((dx + 1) * 3 + dy + 1) * 2 + dz


def axis_rows():
    counter = np.arange(128) % NAXES
    height = 1.0 - (2.0 * counter + 1.0) / NAXES
    radius = np.sqrt(1.0 - height * height)
    rows = np.stack(
        [radius * np.cos(golden * counter), radius * np.sin(golden * counter), height]
    )
    return np.repeat(rows, 8, axis=0).astype(np.float32)


def split2(value):
    high = value.astype(BF).astype(F32)
    return high, (value - high).astype(BF).astype(F32)


def split3(value):
    high = value.astype(BF)
    rest = value - high.astype(F32)
    middle = rest.astype(BF)
    low = (rest - middle.astype(F32)).astype(BF)
    return high, middle, low


def nt(a, b):
    return lax.dot_general(a, b, (((1,), (1,)), ((), ())), preferred_element_type=F32)


def nn(a, b):
    return lax.dot_general(a, b, (((1,), (0,)), ((), ())), preferred_element_type=F32)


def rows_of(ref, row, count):
    return jnp.broadcast_to(ref[pl.ds(row, 1), :], (count, 128))


def rotated(v, u, n):
    w = [v[d] - u[d] for d in range(3)]
    along = (1.0 - turn_cosine) * (n[0] * w[0] + n[1] * w[1] + n[2] * w[2])
    crossed = [
        n[1] * w[2] - n[2] * w[1],
        n[2] * w[0] - n[0] * w[2],
        n[0] * w[1] - n[1] * w[0],
    ]
    return [u[d] + turn_cosine * w[d] + turn_sine * crossed[d] + along * n[d] for d in range(3)]


def kernel(
    sol_rows,
    mig_rows,
    chains,
    shift,
    sol_pos_hbm,
    sol_vel_hbm,
    mig_pos,
    mig_vel,
    bead_pos,
    bead_vel,
    bond_list,
    cell_axis,
    axis_tab,
    off_hbm,
    vel_hbm,
    bpos_out,
    bvel_out,
    sol_pos,
    sol_vel,
    off_out,
    vel_out,
    bond_s,
    lo_s,
    hi_s,
    V_s,
    acc,
    iota_lo,
    iota_hi,
    limit,
    arr_rows,
    row_send,
    bpack,
    mom,
    E_s,
    D_s,
    sx,
    sy,
    sz,
    se,
    rx,
    ry,
    rz,
    re,
    ux,
    uy,
    uz,
    ue,
    gx_,
    gy_,
    gz_,
    ge,
    U_s,
    T_f,
    T_s,
    psend,
    ghost,
    G_s,
    GT_s,
    P_s,
    M_s,
    A_s,
    W_s,
    mig_ss,
    mig_rs,
    halo_ss,
    halo_rs,
    info_ss,
    info_rs,
    bead_ss,
    bead_rs,
    in_sem,
    out_sem,
    entered,
):
    ix = lax.axis_index("gx")
    iy = lax.axis_index("gy")
    iz = lax.axis_index("gz")

    def device(dx, dy, dz):
        return (
            lax.rem(ix + dx + 8, 8),
            lax.rem(iy + dy + 8, 8),
            lax.rem(iz + dz + 2, 2),
        )

    barrier = pltpu.get_barrier_semaphore()

    def tell(sem):
        for off in FACES:
            pl.semaphore_signal(sem, inc=1, device_id=device(*off), device_id_type=MESH)

    tell(barrier)

    HALF = RES // 2

    def in_copies(chunk):
        part = pl.ds(chunk * HALF, HALF)
        return [
            pltpu.make_async_copy(
                sol_pos_hbm.at[:, part], sol_pos.at[:, part], in_sem.at[0, chunk]
            ),
            pltpu.make_async_copy(
                sol_vel_hbm.at[:, part], sol_vel.at[:, part], in_sem.at[1, chunk]
            ),
        ]

    for chunk in range(2):
        for copy in in_copies(chunk):
            copy.start()

    iota_lo[...] = lax.broadcasted_iota(jnp.int32, (256, 128), 0).astype(F32).astype(BF)
    iota_hi[...] = (
        (lax.broadcasted_iota(jnp.int32, (TROWS, 128), 0) // CH).astype(F32).astype(BF)
    )
    acc[...] = jnp.zeros_like(acc)
    bpack[...] = jnp.zeros_like(bpack)
    one16 = jnp.ones((16, 128), BF)
    zero16 = jnp.zeros((16, 128), BF)
    sub8 = lax.broadcasted_iota(jnp.int32, (8, 128), 0)
    lane256 = lax.broadcasted_iota(jnp.int32, (1, 256), 1)
    anchor = [(ix * 16).astype(F32), (iy * 16).astype(F32), (iz * 32).astype(F32)]
    shifts = [shift[d].astype(F32) for d in range(3)]
    bead_live = lane256 < CHAIN * chains[0]
    bond_live = lane256 < (CHAIN - 1) * chains[0]

    start = [bead_pos[d] for d in range(3)]

    def place(exchange, value):
        for d in range(3):
            psend[exchange, d : d + 1, :] = jnp.where(bead_live, value[d], far_point)
        psend[exchange, 3:4, :] = jnp.zeros((1, 256), F32)

    place(0, start)
    for g in range(6):
        row_send[g] = jnp.broadcast_to(mig_rows[g], (1, 128)).astype(jnp.int32)

    def prep(row0, p, v, weight):
        level = []
        for d in range(3):
            level.append(jnp.floor((p[d] * 16.0 + shifts[d]) * 0.0625) - anchor[d])
        lx, ly, lz = level
        xe = lx > 15.5
        ye = ly > 15.5
        ze = lz > 31.5
        zb = jnp.where(lz > 15.5, 1.0, 0.0)
        zm = lz - 16.0 * zb
        both = xe & ye
        edge = xe | ye
        along = jnp.where(xe, ly, lx)
        lo_edge = jnp.where(
            both,
            32.0 + lz,
            jnp.where(ze, along + jnp.where(xe, 0.0, 16.0), along * 16.0 + zm),
        )
        hi_edge = jnp.where(both | ze, 37.0, jnp.where(xe, 33.0, 35.0) + zb)
        lo_s[pl.ds(row0, 8), :] = jnp.where(edge, lo_edge, lx * 16.0 + ly)
        hi_s[pl.ds(row0, 8), :] = jnp.where(edge, hi_edge, lz)
        V_s[pl.ds(row0 * 8, 8, stride=8), :] = weight
        for d in range(3):
            high, low = split2(weight * v[d])
            V_s[pl.ds(row0 * 8 + 1 + d, 8, stride=8), :] = high
            V_s[pl.ds(row0 * 8 + 4 + d, 8, stride=8), :] = low
        V_s[pl.ds(row0 * 8 + 7, 8, stride=8), :] = jnp.zeros((8, 128), F32)

    limit[0 : RES // 8, :] = jnp.broadcast_to(sol_rows[0], (RES // 8, 128)).astype(jnp.int32)

    def solvent(b, i):
        r = pl.multiple_of(b * STEP + 8 * i, 8)
        live = sub8 + r < limit[pl.ds(b * (STEP // 8) + i, 1), :]
        return (
            r,
            [sol_pos[d, pl.ds(r, 8), :] for d in range(3)],
            [sol_vel[d, pl.ds(r, 8), :] for d in range(3)],
            live,
        )

    def prep_step(b):
        for i in range(STEP // 8):
            r, p, v, live = solvent(b, i)
            prep(r, p, v, jnp.where(live, 1.0, 0.0))

    faces = [(-1, 0, 0), (1, 0, 0), (0, -1, 0), (0, 1, 0), (0, 0, 1), (0, 0, 1)]

    def mig_copies(g, f):
        where = dict(device_id=device(*faces[g]), device_id_type=MESH)
        return [
            pltpu.make_async_remote_copy(
                src_ref=mig_pos.at[:, g],
                dst_ref=sol_pos.at[:, pl.ds(RES + FACE * f, FACE)],
                send_sem=mig_ss.at[0, g],
                recv_sem=mig_rs.at[0, f],
                **where,
            ),
            pltpu.make_async_remote_copy(
                src_ref=mig_vel.at[:, g],
                dst_ref=sol_vel.at[:, pl.ds(RES + FACE * f, FACE)],
                send_sem=mig_ss.at[1, g],
                recv_sem=mig_rs.at[1, f],
                **where,
            ),
            pltpu.make_async_remote_copy(
                src_ref=row_send.at[g],
                dst_ref=arr_rows.at[f],
                send_sem=mig_ss.at[2, g],
                recv_sem=mig_rs.at[2, f],
                **where,
            ),
        ]

    def bead_copy(exchange, off, into):
        return pltpu.make_async_remote_copy(
            src_ref=psend.at[exchange],
            dst_ref=ghost.at[exchange, into],
            send_sem=bead_ss.at[exchange, slot(*off)],
            recv_sem=bead_rs.at[exchange, into],
            device_id=device(*off),
            device_id_type=MESH,
        )

    def bead_send(exchange):
        for dx, dy, dz in OFFSETS:
            bead_copy(exchange, (dx, dy, dz), slot(-dx, -dy, dz)).start()

    def bead_arrive(exchange):
        for off in OFFSETS:
            bead_copy(exchange, off, slot(*off)).wait_recv()

    def hot_lo(row):
        lo_b = rows_of(lo_s, row, 16).astype(BF)
        return jnp.concatenate(
            [
                jnp.where(iota_lo[16 * j : 16 * j + 16, :] == lo_b, one16, zero16)
                for j in range(16)
            ],
            0,
        )

    def bin_rows(row0, count):
        spread = []
        hot = []
        for r in range(count):
            row = row0 + r
            hot.append(hot_lo(row))
            v = V_s[pl.ds(pl.multiple_of(row * 8, 8), 8), :]
            v = jnp.concatenate([v, v], 0).astype(BF)
            hi_b = rows_of(hi_s, row, 16).astype(BF)
            spread.append(
                jnp.concatenate(
                    [
                        jnp.where(iota_hi[16 * j : 16 * j + 16, :] == hi_b, v, zero16)
                        for j in range(TROWS // 16)
                    ],
                    0,
                )
            )
        sums = nt(jnp.concatenate(spread, 1), jnp.concatenate(hot, 1))
        acc[0:TROWS, :] += sums[:, 0:128]
        acc[TROWS : 2 * TROWS, :] += sums[:, 128:256]

    for d in range(3):
        for h in range(2):
            half = slice(128 * h, 128 * h + 128)
            bpack[d, h : h + 1, :] = start[d][:, half]
            bpack[3 + d, h : h + 1, :] = bead_vel[d][:, half]
    lane8 = lax.broadcasted_iota(jnp.int32, (8, 128), 1) + 128 * sub8
    bead_here = (lane8 < CHAIN * chains[0]) & (sub8 < 2)
    prep(
        SOLV,
        [bpack[d] for d in range(3)],
        [bpack[3 + d] for d in range(3)],
        jnp.where(bead_here, bead_mass, 0.0),
    )
    bin_rows(SOLV, 2)
    RSTEPS = RES // STEP
    HSTEPS = RSTEPS // 2

    STEPS = SOLV // STEP
    for copy in in_copies(0):
        copy.wait()
    prep_step(0)

    def bin_loop(b, carry):
        @pl.when(b == 2)
        def _():
            pl.semaphore_wait(barrier, len(FACES))
            for g in (4, 5, 0, 1, 2, 3):
                for copy in mig_copies(g, g ^ 1):
                    copy.start()
            tell(entered.at[0])

        @pl.when(b == HSTEPS - 1)
        def _():
            for copy in in_copies(1):
                copy.wait()

        @pl.when(b == HSTEPS)
        def _():
            pl.semaphore_wait(entered.at[0], len(FACES))
            tell(entered.at[1])

        @pl.when(b == HSTEPS + 2)
        def _():
            pl.semaphore_wait(entered.at[1], len(FACES))
            bead_send(0)

        for pair in range(3):

            @pl.when(b == RSTEPS - 1 + pair)
            def _():
                for f in (2 * pair, 2 * pair + 1):
                    for copy in mig_copies(f, f):
                        copy.wait_recv()
                    first = (RES + FACE * f) // 8
                    limit[first : first + FACE // 8, :] = (
                        jnp.broadcast_to(arr_rows[f], (FACE // 8, 128)) + RES + FACE * f
                    )

        bin_rows(pl.multiple_of(b * STEP, 8), STEP)
        prep_step(jnp.minimum(b + 1, STEPS - 1))
        return carry

    lax.fori_loop(0, STEPS, bin_loop, 0)

    for c in range(4):
        for h in range(2):
            value = acc[pl.ds(h * TROWS + c, LEVELS, stride=8), :]
            if c > 0:
                value += acc[pl.ds(h * TROWS + c + 3, LEVELS, stride=8), :]
            mom[c, 0:LEVELS, 128 * h : 128 * h + 128] = value
    for c in range(4):
        sz[c : c + 1, :] = mom[c, 32:33, :]
        sx[2 * c : 2 * c + 2, :] = mom[c, 33:35, :]
        sy[2 * c : 2 * c + 2, :] = mom[c, 35:37, :]
        se[c : c + 1, :] = mom[c, 37:38, :]

    def halo_copies(src, dst, ss, rs, sign):
        copies = []
        for i, (dx, dy, dz) in enumerate(HALO):
            s = src[min(i, 3)]
            t = dst[i] if i < 3 else dst[3].at[i - 3]
            copies.append(
                pltpu.make_async_remote_copy(
                    src_ref=s,
                    dst_ref=t,
                    send_sem=ss.at[i],
                    recv_sem=rs.at[i],
                    device_id=device(sign * dx, sign * dy, dz),
                    device_id_type=MESH,
                )
            )
        return copies

    halo = halo_copies((sx, sy, sz, se), (rx, ry, rz, re), halo_ss, halo_rs, 1)
    for copy in halo:
        copy.start()

    row32 = lax.broadcasted_iota(jnp.int32, (32, 256), 0)
    col32 = lax.broadcasted_iota(jnp.int32, (32, 256), 1)
    mask_face = (col32 % 16) == (row32 % 16)
    mask_edge = (
        ((col32 < 32) & (row32 == 0))
        | ((col32 >= 32) & (col32 < 64) & (col32 - 32 == row32))
        | ((col32 == 64) & (row32 == 0))
    )
    er = lax.broadcasted_iota(jnp.int32, (256, 256), 0)
    ec = lax.broadcasted_iota(jnp.int32, (256, 256), 1)

    def as_bf(mask):
        return jnp.where(mask, 1.0, 0.0).astype(BF)

    E_s[0:256, :] = as_bf(ec == er // 16)
    E_s[256:512, :] = as_bf(ec == (er // 16) * 16)
    target = jnp.where(er < 16, er, jnp.where(er < 32, (er - 16) * 16, 0))
    E_s[512:768, :] = as_bf(ec == target)
    bond_s[:, :, 0:BONDS] = bond_list[...]
    first = jnp.where(bond_live, bond_s[0], -1)
    second = jnp.where(bond_live, bond_s[1], -1)
    D_s[...] = (
        jnp.where(er == first, 1.0, 0.0) - jnp.where(er == second, 1.0, 0.0)
    ).astype(BF)

    row_c = lax.broadcasted_iota(jnp.int32, (72, 256), 0)
    block = row_c // 4
    comp = row_c % 4
    bx = block // 6 - 1
    by = (block // 2) % 3 - 1
    wrap_x = jnp.where(ix + bx < 0, -128.0, jnp.where(ix + bx > 7, 128.0, 0.0))
    wrap_y = jnp.where(iy + by < 0, -128.0, jnp.where(iy + by > 7, 128.0, 0.0))
    image = jnp.where(comp == 0, wrap_x, jnp.where(comp == 1, wrap_y, 0.0))
    wrapped = (comp == 2) & (block % 2 == 1)
    centre = anchor[2] + 16.0
    upper = ((comp == 0) & (bx == 1)) | ((comp == 1) & (by == 1))
    G_s[...] = jnp.zeros_like(G_s)

    def forces(exchange):
        own = slot(0, 0, 0)
        for k in range(18):
            if k == own:
                G_s[0:4, :] = psend[exchange]
                P_s[4 * k : 4 * k + 4, :] = psend[exchange]
            else:
                P_s[4 * k : 4 * k + 4, :] = ghost[exchange, k]
        GT_s[...] = G_s[...].T
        at = P_s[...] + image
        turns = jnp.floor((at - centre) * (1.0 / 64.0) + 0.5)
        at = jnp.where(wrapped, at - 64.0 * turns, at)
        at = jnp.where(upper & (at < -500.0), -3.0 * far_point, at)
        P_s[...] = at
        M_s[0:24, :] = 0.5 * (at[0:24] + at[48:72])
        M_s[24:32, :] = 0.5 * (at[24:32] + at[40:48])

        def group(j, carry):
            here = []
            for t in range(2):
                tile = GT_s[pl.ds(pl.multiple_of(16 * j + 8 * t, 8), 8), :]
                here.append([jnp.broadcast_to(tile[:, d : d + 1], (8, 128)) for d in range(3)])
            twice = [here[t][1] + here[t][1] for t in range(2)]
            sums = [jnp.zeros((8, 128), F32) for i in range(6)]

            def choose(mask, a, b):
                return [jnp.where(mask, a[d], b[d]) for d in range(3)]

            def add(t, other):
                differ = [here[t][d] - other[d] for d in range(3)]
                square = differ[0] * differ[0] + differ[1] * differ[1] + differ[2] * differ[2]
                inverse = 1.0 / jnp.where(square > 0.25, square, 1.0e6)
                sixth = inverse * inverse * inverse
                weight = jnp.maximum(48.0 * sixth - 24.0, 0.0) * sixth * inverse
                for d in range(3):
                    sums[3 * t + d] = sums[3 * t + d] + weight * differ[d]

            for h in range(2):
                half = slice(128 * h, 128 * h + 128)

                def row(ref, r):
                    return jnp.broadcast_to(ref[r : r + 1, half], (8, 128))

                def ghost_at(dx, dy, dz):
                    return [row(P_s, 4 * slot(dx, dy, dz) + d) for d in range(3)]

                for dz in (0, 1):
                    inner = ghost_at(0, 0, dz)
                    for t in range(2):
                        add(t, inner)
                    low, high = ghost_at(0, -1, dz), ghost_at(0, 1, dz)
                    half_way = row(M_s, 4 * slot(0, -1, dz) + 1)
                    for t in range(2):
                        add(t, choose(here[t][1] < half_way, low, high))
                    near = [[], []]
                    for dy in (0, -1, 1):
                        low, high = ghost_at(-1, dy, dz), ghost_at(1, dy, dz)
                        half_way = row(M_s, 4 * slot(-1, dy, dz))
                        for t in range(2):
                            near[t].append(choose(here[t][0] < half_way, low, high))
                    for t in range(2):
                        side, low, high = near[t]
                        add(t, side)
                        add(t, choose(twice[t] < low[1] + high[1], low, high))
            for t in range(2):
                for d in range(3):
                    A_s[pl.ds(pl.multiple_of(256 * d + 16 * j + 8 * t, 8), 8), :] = sums[3 * t + d]
            return carry

        lax.fori_loop(0, 16, group, 0)
        ones = jnp.ones((8, 128), BF)
        pieces = split3(A_s[...])
        pair = nt(ones, pieces[0]) + nt(ones, pieces[1]) + nt(ones, pieces[2])
        pieces = split3(jnp.concatenate([psend[exchange], psend[exchange]], 0))
        hot = D_s[...]
        differ = nn(pieces[0], hot) + nn(pieces[1], hot) + nn(pieces[2], hot)
        square = jnp.sum(jnp.where(sub256 < 3, differ * differ, 0.0), axis=0, keepdims=True)
        weight = jnp.where(bond_live, -spring / (1.0 - square / reach_square), 0.0)
        pieces = split3(weight * differ)
        pull = nt(pieces[0], hot) + nt(pieces[1], hot) + nt(pieces[2], hot)
        return [pair[0:1, 256 * d : 256 * d + 256] + pull[d : d + 1, :] for d in range(3)]

    sub256 = lax.broadcasted_iota(jnp.int32, (8, 256), 0)
    bead_arrive(0)
    push = forces(0)

    for copy in halo_copies((sx, sy, sz, se), (rx, ry, rz, re), halo_ss, halo_rs, -1):
        copy.wait_recv()
    zero_face = jnp.zeros((32, 256), F32)
    spread = []
    for c in range(4):
        edge = jnp.where(
            lane256 < 16,
            re[0, c : c + 1, :],
            jnp.where(
                lane256 < 32,
                re[1, c : c + 1, :],
                jnp.where(lane256 < 64, re[2, c : c + 1, :], re[3, c : c + 1, :]),
            ),
        )
        low_half = row32 < 16
        vx = jnp.where(low_half, rx[2 * c : 2 * c + 1, :], rx[2 * c + 1 : 2 * c + 2, :])
        vy = jnp.where(low_half, ry[2 * c : 2 * c + 1, :], ry[2 * c + 1 : 2 * c + 2, :])
        spread.append(
            jnp.concatenate(
                [
                    jnp.where(mask_face, vx, zero_face),
                    jnp.where(mask_face, vy, zero_face),
                    jnp.where(mask_edge, edge, zero_face),
                ],
                1,
            )
        )
    pieces = split3(jnp.concatenate(spread, 0))
    moved = nn(pieces[0], E_s[...]) + nn(pieces[1], E_s[...]) + nn(pieces[2], E_s[...])
    total = []
    for c in range(4):
        value = mom[c, 0:32, :] + moved[32 * c : 32 * c + 32, :]
        total.append(value + jnp.where(row32 == 0, rz[c : c + 1, :], 0.0))
    scale = 1.0 / jnp.maximum(total[0], 1.0)
    eye = (
        lax.broadcasted_iota(jnp.int32, (32, 32), 0) == lax.broadcasted_iota(jnp.int32, (32, 32), 1)
    )
    axis_here = nt(as_bf(eye), cell_axis[...].astype(F32).astype(BF))
    parts = [None] * 8
    for d in range(3):
        parts[d], parts[3 + d] = split2(total[1 + d] * scale)
    parts[6] = axis_here
    parts[7] = zero_face
    for c in range(8):
        for h in range(2):
            T_f[pl.ds(h * TROWS + c, 32, stride=8), :] = parts[c][:, 128 * h : 128 * h + 128]
    picked = nt(jnp.concatenate(parts[:7], 0).astype(BF), E_s[...])
    for q in range(4):
        if q < 3:
            value = picked[32 * q : 32 * q + 32, :] + picked[96 + 32 * q : 128 + 32 * q, :]
            uz[q : q + 1, :] = parts[q][0:1, :] + parts[3 + q][0:1, :]
        else:
            value = picked[192:224, :]
            uz[q : q + 1, :] = parts[6][0:1, :]
        vx = jnp.where(mask_face, value[:, 0:256], 0.0)
        vy = jnp.where(mask_face, value[:, 256:512], 0.0)
        ve = jnp.where(mask_edge, value[:, 512:768], 0.0)
        for j in range(2):
            half = slice(16 * j, 16 * j + 16)
            ux[2 * q + j : 2 * q + j + 1, :] = jnp.sum(vx[half], axis=0, keepdims=True)
            uy[2 * q + j : 2 * q + j + 1, :] = jnp.sum(vy[half], axis=0, keepdims=True)
        ue[q : q + 1, :] = jnp.sum(ve, axis=0, keepdims=True)
    info = halo_copies((ux, uy, uz, ue), (gx_, gy_, gz_, ge), info_ss, info_rs, -1)
    for copy in info:
        copy.start()
    for copy in halo_copies((ux, uy, uz, ue), (gx_, gy_, gz_, ge), info_ss, info_rs, 1):
        copy.wait_recv()

    def halo_level(level, channel, value):
        for h in range(2):
            row = h * TROWS + 8 * level + channel
            T_f[row : row + 1, :] = value[:, 128 * h : 128 * h + 128]

    for q in range(4):
        edge = jnp.where(
            lane256 < 16,
            ge[0, q : q + 1, :],
            jnp.where(
                lane256 < 32,
                ge[1, q : q + 1, :],
                jnp.where(lane256 < 64, ge[2, q : q + 1, :], ge[3, q : q + 1, :]),
            ),
        )
        edge = jnp.where(lane256 < 65, edge, 0.0)
        values = [gz_[q : q + 1, :]]
        values += [gx_[2 * q + j : 2 * q + j + 1, :] for j in range(2)]
        values += [gy_[2 * q + j : 2 * q + j + 1, :] for j in range(2)]
        values += [edge]
        for i, value in enumerate(values):
            if q < 3:
                high, low = split2(value)
                halo_level(32 + i, q, high)
                halo_level(32 + i, 3 + q, low)
            else:
                halo_level(32 + i, 6, value)
                halo_level(32 + i, 7, jnp.zeros((1, 256), F32))
    for h in range(2):
        half = slice(128 * h, 128 * h + 128)
        T_s[:, half] = T_f[h * TROWS : h * TROWS + TROWS, :].astype(BF)

    def look_rows(row0, count):
        hot = jnp.concatenate([hot_lo(row0 + r) for r in range(count)], 1)
        found = nn(T_s[...], hot)
        for r in range(count):
            row = row0 + r
            level = rows_of(hi_s, row, 8).astype(jnp.int32)
            values = [
                found[8 * j : 8 * j + 8, 128 * r : 128 * r + 128] for j in range(LEVELS)
            ]
            bit = 1
            while len(values) > 1:
                odd = (level & bit) != 0
                values = [
                    jnp.where(odd, values[i + 1], values[i]) if i + 1 < len(values) else values[i]
                    for i in range(0, len(values), 2)
                ]
                bit = 2 * bit
            V_s[pl.ds(pl.multiple_of(row * 8, 8), 8), :] = values[0]

    def collide(row0, v):
        read = [V_s[pl.ds(row0 * 8 + c, 8, stride=8), :] for c in range(7)]
        u = [read[d] + read[3 + d] for d in range(3)]
        index = read[6].astype(jnp.int32)
        n = [
            jnp.take_along_axis(axis_tab[8 * d : 8 * d + 8, :], index, axis=1) for d in range(3)
        ]
        return rotated(v, u, n)

    def emit(row0, p, v, live):
        new = collide(row0, v)
        for d in range(3):
            offset = p[d] - jnp.floor(p[d]) - 0.5
            vel_out[d, pl.ds(row0, 8), :] = new[d]
            off_out[d, pl.ds(row0, 8), :] = jnp.where(live, offset, 2.0)

    def emit_step(b):
        for i in range(STEP // 8):
            emit(*solvent(b, i))

    def look_loop(b, carry):
        emit_step(jnp.maximum(b - 1, 0))
        look_rows(pl.multiple_of(b * STEP, 8), STEP)
        return carry

    look_rows(SOLV, 2)
    new = collide(SOLV, [bpack[3 + d] for d in range(3)])
    speed = []
    for d in range(3):
        W_s[d] = new[d]
        speed.append(jnp.concatenate([W_s[d, 0:1, :], W_s[d, 1:2, :]], 1))

    def out_copies(part):
        rows = pl.ds(part * HALF, HALF) if part < 2 else pl.ds(RES, SOLV - RES)
        return [
            pltpu.make_async_copy(
                off_out.at[:, rows], off_hbm.at[:, rows], out_sem.at[0, part]
            ),
            pltpu.make_async_copy(
                vel_out.at[:, rows], vel_hbm.at[:, rows], out_sem.at[1, part]
            ),
        ]

    half_kick = 0.5 * step_size / bead_mass

    def substep(t, carry):
        speed, gone, push = carry[0:3], carry[3:6], carry[6:9]
        speed = [speed[d] + half_kick * push[d] for d in range(3)]
        gone = [gone[d] + step_size * speed[d] for d in range(3)]
        place(t + 1, [start[d] + gone[d] for d in range(3)])
        bead_send(t + 1)
        lax.fori_loop(
            HSTEPS * t, jnp.minimum(HSTEPS * (t + 1), STEPS), look_loop, 0
        )

        @pl.when(t == 1)
        def _():
            for copy in out_copies(0):
                copy.start()

        @pl.when(t == 2)
        def _():
            emit_step(STEPS - 1)
            for part in (1, 2):
                for copy in out_copies(part):
                    copy.start()

        bead_arrive(t + 1)
        push = forces(t + 1)
        speed = [speed[d] + half_kick * push[d] for d in range(3)]
        return (*speed, *gone, *push)

    still = jnp.zeros((1, 256), F32)
    last = lax.fori_loop(0, 3, substep, (*speed, still, still, still, *push))
    for d in range(3):
        bpos_out[d] = last[3 + d]
        bvel_out[d] = last[d]
    for part in range(3):
        for copy in out_copies(part):
            copy.wait()

    for g in range(6):
        for copy in mig_copies(g, g ^ 1):
            copy.wait_send()
    for copy in halo:
        copy.wait_send()
    for copy in info:
        copy.wait_send()
    for exchange in range(4):
        for dx, dy, dz in OFFSETS:
            bead_copy(exchange, (dx, dy, dz), slot(-dx, -dy, dz)).wait_send()


def shards(
    sol_pos,
    sol_vel,
    sol_rows,
    mig_pos,
    mig_vel,
    mig_rows,
    bead_pos,
    bead_vel,
    bead_chains,
    bond_list,
    cell_axis,
    shift,
):
    vmem = pl.BlockSpec(memory_space=pltpu.VMEM)
    smem = pl.BlockSpec(memory_space=pltpu.SMEM)
    anywhere = pl.BlockSpec(memory_space=pl.ANY)
    dma = pltpu.SemaphoreType.DMA
    f32 = lambda *shape: pltpu.VMEM(shape, F32)
    bf = lambda *shape: pltpu.VMEM(shape, BF)
    outs = pl.pallas_call(
        kernel,
        out_shape=(
            jax.ShapeDtypeStruct((3, SOLV, 128), F32),
            jax.ShapeDtypeStruct((3, SOLV, 128), F32),
            jax.ShapeDtypeStruct((3, 1, BEADS), F32),
            jax.ShapeDtypeStruct((3, 1, BEADS), F32),
        ),
        in_specs=[smem] * 4 + [anywhere] * 4 + [vmem] * 5,
        out_specs=(anywhere, anywhere, vmem, vmem),
        scratch_shapes=[
            f32(3, SOLV, 128),
            f32(3, SOLV, 128),
            f32(3, SOLV, 128),
            f32(3, SOLV, 128),
            pltpu.VMEM((2, 1, 256), jnp.int32),
            f32(ALL, 128),
            f32(ALL, 128),
            f32(ALL * 8, 128),
            f32(2 * TROWS, 128),
            bf(256, 128),
            bf(TROWS, 128),
            pltpu.VMEM((72, 128), jnp.int32),
            pltpu.VMEM((6, 1, 128), jnp.int32),
            pltpu.VMEM((6, 1, 128), jnp.int32),
            f32(6, 8, 128),
            f32(4, 40, 256),
            bf(768, 256),
            bf(256, 256),
            f32(8, 256),
            f32(8, 256),
            f32(4, 256),
            f32(4, 256),
            f32(8, 256),
            f32(8, 256),
            f32(4, 256),
            f32(4, 4, 256),
            f32(8, 256),
            f32(8, 256),
            f32(4, 256),
            f32(4, 256),
            f32(8, 256),
            f32(8, 256),
            f32(4, 256),
            f32(4, 4, 256),
            f32(4, 32, 256),
            f32(2 * TROWS, 128),
            bf(TROWS, 256),
            f32(4, 4, 256),
            f32(4, 18, 4, 256),
            f32(128, 256),
            f32(256, 128),
            f32(72, 256),
            f32(32, 256),
            f32(768, 128),
            f32(3, 8, 128),
            dma((3, 6)),
            dma((3, 6)),
            dma((7,)),
            dma((7,)),
            dma((7,)),
            dma((7,)),
            dma((4, 18)),
            dma((4, 18)),
            dma((2, 2)),
            dma((2, 3)),
            pltpu.SemaphoreType.REGULAR((2,)),
        ],
        compiler_params=pltpu.CompilerParams(
            collective_id=0, has_side_effects=True, vmem_limit_bytes=60 * 1024 * 1024
        ),
        name="interval",
    )(
        sol_rows.reshape(1),
        mig_rows.reshape(6),
        bead_chains.reshape(1),
        shift,
        sol_pos.reshape(3, RES, 128),
        sol_vel.reshape(3, RES, 128),
        mig_pos.reshape(3, 6, FACE, 128),
        mig_vel.reshape(3, 6, FACE, 128),
        bead_pos.reshape(3, 1, BEADS),
        bead_vel.reshape(3, 1, BEADS),
        bond_list.reshape(2, 1, BONDS),
        cell_axis.reshape(256, 32),
        jnp.asarray(axis_rows()),
    )
    offset, vel, bpos, bvel = outs
    live = offset < 1.0
    bead_live = jnp.arange(BEADS, dtype=jnp.int32) < CHAIN * bead_chains.reshape(())
    return (
        jnp.where(live, offset + 3.0 * step_size * vel, 0.0).reshape(3, 1, 1, 1, SOLV * 128),
        jnp.where(live, vel, 0.0).reshape(3, 1, 1, 1, SOLV * 128),
        jnp.where(bead_live, bpos, 0.0).reshape(3, 1, 1, 1, BEADS),
        jnp.where(bead_live, bvel, 0.0).reshape(3, 1, 1, 1, BEADS),
    )


def solution(mesh):
    return jax.shard_map(
        shards,
        mesh=mesh,
        in_specs=(
            P(None, "gx", "gy", "gz", None),
            P(None, "gx", "gy", "gz", None),
            P("gx", "gy", "gz"),
            P(None, "gx", "gy", "gz", None, None),
            P(None, "gx", "gy", "gz", None, None),
            P("gx", "gy", "gz", None),
            P(None, "gx", "gy", "gz", None),
            P(None, "gx", "gy", "gz", None),
            P("gx", "gy", "gz"),
            P(None, "gx", "gy", "gz", None),
            P("gx", "gy", "gz"),
            P(),
        ),
        out_specs=(
            P(None, "gx", "gy", "gz", None),
            P(None, "gx", "gy", "gz", None),
            P(None, "gx", "gy", "gz", None),
            P(None, "gx", "gy", "gz", None),
        ),
        check_vma=False,
    )
```

```python
import math

import jax
import jax.numpy as jnp
import numpy as np
from jax import lax
from jax.experimental import pallas as pl
from jax.experimental.pallas import tpu as pltpu
from jax.sharding import PartitionSpec as P

BF = jnp.bfloat16
F32 = jnp.float32
MESH = pl.DeviceIdType.MESH

UNITS = 16
NAXES = 32
CHAIN = 8
bead_mass = 5.0
step_size = 0.02
spring = 30.0
reach_square = 2.25
far_point = -1000.0
cut_square = 2.0 ** (1.0 / 3.0)
turn_cosine = math.cos(130.0 * math.pi / 180.0)
turn_sine = math.sin(130.0 * math.pi / 180.0)
golden = math.pi * (3.0 - math.sqrt(5.0))

LANES = 256
LEVELS = 38
CH = 8
TROWS = LEVELS * CH
RES = 384
FACE = 24
SOLV = RES + 6 * FACE
ALL = SOLV + 8
STEP = 2 * FACE
BEADS = 256
BONDS = 224

OFFSETS = [
    (dx, dy, dz)
    for dx in (-1, 0, 1)
    for dy in (-1, 0, 1)
    for dz in (0, 1)
    if (dx, dy, dz) != (0, 0, 0)
]
OFFSETS.sort(key=lambda off: -(abs(off[0]) + abs(off[1]) + 2 * off[2]))
FACES = [(-1, 0, 0), (1, 0, 0), (0, -1, 0), (0, 1, 0), (0, 0, 1)]
HALO = [(1, 0, 0), (0, 1, 0), (0, 0, 1), (1, 0, 1), (0, 1, 1), (1, 1, 0), (1, 1, 1)]


def slot(dx, dy, dz):
    return ((dx + 1) * 3 + dy + 1) * 2 + dz


def axis_rows():
    counter = np.arange(128) % NAXES
    height = 1.0 - (2.0 * counter + 1.0) / NAXES
    radius = np.sqrt(1.0 - height * height)
    rows = np.stack(
        [radius * np.cos(golden * counter), radius * np.sin(golden * counter), height]
    )
    return np.repeat(rows, 8, axis=0).astype(np.float32)


def split2(value):
    high = value.astype(BF).astype(F32)
    return high, (value - high).astype(BF).astype(F32)


def split3(value):
    high = value.astype(BF)
    rest = value - high.astype(F32)
    middle = rest.astype(BF)
    low = (rest - middle.astype(F32)).astype(BF)
    return high, middle, low


def nt(a, b):
    return lax.dot_general(a, b, (((1,), (1,)), ((), ())), preferred_element_type=F32)


def nn(a, b):
    return lax.dot_general(a, b, (((1,), (0,)), ((), ())), preferred_element_type=F32)


def rows_of(ref, row, count):
    return jnp.broadcast_to(ref[pl.ds(row, 1), :], (count, 128))


def rotated(v, u, n):
    w = [v[d] - u[d] for d in range(3)]
    along = (1.0 - turn_cosine) * (n[0] * w[0] + n[1] * w[1] + n[2] * w[2])
    crossed = [
        n[1] * w[2] - n[2] * w[1],
        n[2] * w[0] - n[0] * w[2],
        n[0] * w[1] - n[1] * w[0],
    ]
    return [u[d] + turn_cosine * w[d] + turn_sine * crossed[d] + along * n[d] for d in range(3)]


def kernel(
    sol_rows,
    mig_rows,
    chains,
    shift,
    sol_pos_hbm,
    sol_vel_hbm,
    mig_pos,
    mig_vel,
    bead_pos,
    bead_vel,
    bond_list,
    cell_axis,
    axis_tab,
    off_hbm,
    vel_hbm,
    bpos_out,
    bvel_out,
    sol_pos,
    sol_vel,
    off_out,
    vel_out,
    bond_s,
    lo_s,
    hi_s,
    V_s,
    acc,
    iota_lo,
    iota_hi,
    limit,
    arr_rows,
    row_send,
    bpack,
    mom,
    E_s,
    D_s,
    sx,
    sy,
    sz,
    se,
    rx,
    ry,
    rz,
    re,
    ux,
    uy,
    uz,
    ue,
    gx_,
    gy_,
    gz_,
    ge,
    U_s,
    T_f,
    T_s,
    psend,
    ghost,
    G_s,
    GT_s,
    P_s,
    M_s,
    A_s,
    W_s,
    mig_ss,
    mig_rs,
    halo_ss,
    halo_rs,
    info_ss,
    info_rs,
    bead_ss,
    bead_rs,
    in_sem,
    out_sem,
    entered,
):
    ix = lax.axis_index("gx")
    iy = lax.axis_index("gy")
    iz = lax.axis_index("gz")

    def device(dx, dy, dz):
        return (
            lax.rem(ix + dx + 8, 8),
            lax.rem(iy + dy + 8, 8),
            lax.rem(iz + dz + 2, 2),
        )

    barrier = pltpu.get_barrier_semaphore()

    def tell(sem):
        for off in FACES:
            pl.semaphore_signal(sem, inc=1, device_id=device(*off), device_id_type=MESH)

    tell(barrier)

    HALF = RES // 2

    def in_copies(chunk):
        part = pl.ds(chunk * HALF, HALF)
        return [
            pltpu.make_async_copy(
                sol_pos_hbm.at[:, part], sol_pos.at[:, part], in_sem.at[0, chunk]
            ),
            pltpu.make_async_copy(
                sol_vel_hbm.at[:, part], sol_vel.at[:, part], in_sem.at[1, chunk]
            ),
        ]

    for chunk in range(2):
        for copy in in_copies(chunk):
            copy.start()

    iota_lo[...] = lax.broadcasted_iota(jnp.int32, (256, 128), 0).astype(F32).astype(BF)
    iota_hi[...] = (
        (lax.broadcasted_iota(jnp.int32, (TROWS, 128), 0) // CH).astype(F32).astype(BF)
    )
    acc[...] = jnp.zeros_like(acc)
    bpack[...] = jnp.zeros_like(bpack)
    one16 = jnp.ones((16, 128), BF)
    zero16 = jnp.zeros((16, 128), BF)
    sub8 = lax.broadcasted_iota(jnp.int32, (8, 128), 0)
    lane256 = lax.broadcasted_iota(jnp.int32, (1, 256), 1)
    anchor = [(ix * 16).astype(F32), (iy * 16).astype(F32), (iz * 32).astype(F32)]
    shifts = [shift[d].astype(F32) for d in range(3)]
    bead_live = lane256 < CHAIN * chains[0]
    bond_live = lane256 < (CHAIN - 1) * chains[0]

    start = [bead_pos[d] for d in range(3)]

    def place(exchange, value):
        for d in range(3):
            psend[exchange, d : d + 1, :] = jnp.where(bead_live, value[d], far_point)
        psend[exchange, 3:4, :] = jnp.zeros((1, 256), F32)

    place(0, start)
    for g in range(6):
        row_send[g] = jnp.broadcast_to(mig_rows[g], (1, 128)).astype(jnp.int32)

    def prep(row0, p, v, weight):
        level = []
        for d in range(3):
            level.append(jnp.floor((p[d] * 16.0 + shifts[d]) * 0.0625) - anchor[d])
        lx, ly, lz = level
        xe = lx > 15.5
        ye = ly > 15.5
        ze = lz > 31.5
        zb = jnp.where(lz > 15.5, 1.0, 0.0)
        zm = lz - 16.0 * zb
        both = xe & ye
        edge = xe | ye
        along = jnp.where(xe, ly, lx)
        lo_edge = jnp.where(
            both,
            32.0 + lz,
            jnp.where(ze, along + jnp.where(xe, 0.0, 16.0), along * 16.0 + zm),
        )
        hi_edge = jnp.where(both | ze, 37.0, jnp.where(xe, 33.0, 35.0) + zb)
        lo_s[pl.ds(row0, 8), :] = jnp.where(edge, lo_edge, lx * 16.0 + ly)
        hi_s[pl.ds(row0, 8), :] = jnp.where(edge, hi_edge, lz)
        V_s[pl.ds(row0 * 8, 8, stride=8), :] = weight
        for d in range(3):
            high, low = split2(weight * v[d])
            V_s[pl.ds(row0 * 8 + 1 + d, 8, stride=8), :] = high
            V_s[pl.ds(row0 * 8 + 4 + d, 8, stride=8), :] = low
        V_s[pl.ds(row0 * 8 + 7, 8, stride=8), :] = jnp.zeros((8, 128), F32)

    limit[0 : RES // 8, :] = jnp.broadcast_to(sol_rows[0], (RES // 8, 128)).astype(jnp.int32)

    def solvent(b, i):
        r = pl.multiple_of(b * STEP + 8 * i, 8)
        live = sub8 + r < limit[pl.ds(b * (STEP // 8) + i, 1), :]
        return (
            r,
            [sol_pos[d, pl.ds(r, 8), :] for d in range(3)],
            [sol_vel[d, pl.ds(r, 8), :] for d in range(3)],
            live,
        )

    def prep_step(b):
        for i in range(STEP // 8):
            r, p, v, live = solvent(b, i)
            prep(r, p, v, jnp.where(live, 1.0, 0.0))

    faces = [(-1, 0, 0), (1, 0, 0), (0, -1, 0), (0, 1, 0), (0, 0, 1), (0, 0, 1)]

    def mig_copies(g, f):
        where = dict(device_id=device(*faces[g]), device_id_type=MESH)
        return [
            pltpu.make_async_remote_copy(
                src_ref=mig_pos.at[:, g],
                dst_ref=sol_pos.at[:, pl.ds(RES + FACE * f, FACE)],
                send_sem=mig_ss.at[0, g],
                recv_sem=mig_rs.at[0, f],
                **where,
            ),
            pltpu.make_async_remote_copy(
                src_ref=mig_vel.at[:, g],
                dst_ref=sol_vel.at[:, pl.ds(RES + FACE * f, FACE)],
                send_sem=mig_ss.at[1, g],
                recv_sem=mig_rs.at[1, f],
                **where,
            ),
            pltpu.make_async_remote_copy(
                src_ref=row_send.at[g],
                dst_ref=arr_rows.at[f],
                send_sem=mig_ss.at[2, g],
                recv_sem=mig_rs.at[2, f],
                **where,
            ),
        ]

    def bead_copy(exchange, off, into):
        return pltpu.make_async_remote_copy(
            src_ref=psend.at[exchange],
            dst_ref=ghost.at[exchange, into],
            send_sem=bead_ss.at[exchange, slot(*off)],
            recv_sem=bead_rs.at[exchange, into],
            device_id=device(*off),
            device_id_type=MESH,
        )

    def bead_send(exchange):
        for dx, dy, dz in OFFSETS:
            bead_copy(exchange, (dx, dy, dz), slot(-dx, -dy, dz)).start()

    def bead_arrive(exchange):
        for off in OFFSETS:
            bead_copy(exchange, off, slot(*off)).wait_recv()

    def hot_lo(row):
        lo_b = rows_of(lo_s, row, 16).astype(BF)
        return jnp.concatenate(
            [
                jnp.where(iota_lo[16 * j : 16 * j + 16, :] == lo_b, one16, zero16)
                for j in range(16)
            ],
            0,
        )

    def bin_rows(row0, count):
        spread = []
        hot = []
        for r in range(count):
            row = row0 + r
            hot.append(hot_lo(row))
            v = V_s[pl.ds(pl.multiple_of(row * 8, 8), 8), :]
            v = jnp.concatenate([v, v], 0).astype(BF)
            hi_b = rows_of(hi_s, row, 16).astype(BF)
            spread.append(
                jnp.concatenate(
                    [
                        jnp.where(iota_hi[16 * j : 16 * j + 16, :] == hi_b, v, zero16)
                        for j in range(TROWS // 16)
                    ],
                    0,
                )
            )
        sums = nt(jnp.concatenate(spread, 1), jnp.concatenate(hot, 1))
        acc[0:TROWS, :] += sums[:, 0:128]
        acc[TROWS : 2 * TROWS, :] += sums[:, 128:256]

    for d in range(3):
        for h in range(2):
            half = slice(128 * h, 128 * h + 128)
            bpack[d, h : h + 1, :] = start[d][:, half]
            bpack[3 + d, h : h + 1, :] = bead_vel[d][:, half]
    lane8 = lax.broadcasted_iota(jnp.int32, (8, 128), 1) + 128 * sub8
    bead_here = (lane8 < CHAIN * chains[0]) & (sub8 < 2)
    prep(
        SOLV,
        [bpack[d] for d in range(3)],
        [bpack[3 + d] for d in range(3)],
        jnp.where(bead_here, bead_mass, 0.0),
    )
    bin_rows(SOLV, 2)
    RSTEPS = RES // STEP
    HSTEPS = RSTEPS // 2

    STEPS = SOLV // STEP
    for copy in in_copies(0):
        copy.wait()
    prep_step(0)

    def bin_loop(b, carry):
        @pl.when(b == 2)
        def _():
            pl.semaphore_wait(barrier, len(FACES))
            for g in (4, 5, 0, 1, 2, 3):
                for copy in mig_copies(g, g ^ 1):
                    copy.start()
            tell(entered.at[0])

        @pl.when(b == HSTEPS - 1)
        def _():
            for copy in in_copies(1):
                copy.wait()

        @pl.when(b == HSTEPS)
        def _():
            pl.semaphore_wait(entered.at[0], len(FACES))
            tell(entered.at[1])

        @pl.when(b == HSTEPS + 2)
        def _():
            pl.semaphore_wait(entered.at[1], len(FACES))
            bead_send(0)

        for pair in range(3):

            @pl.when(b == RSTEPS - 1 + pair)
            def _():
                for f in (2 * pair, 2 * pair + 1):
                    for copy in mig_copies(f, f):
                        copy.wait_recv()
                    first = (RES + FACE * f) // 8
                    limit[first : first + FACE // 8, :] = (
                        jnp.broadcast_to(arr_rows[f], (FACE // 8, 128)) + RES + FACE * f
                    )

        bin_rows(pl.multiple_of(b * STEP, 8), STEP)
        prep_step(jnp.minimum(b + 1, STEPS - 1))
        return carry

    lax.fori_loop(0, STEPS, bin_loop, 0)

    for c in range(4):
        for h in range(2):
            value = acc[pl.ds(h * TROWS + c, LEVELS, stride=8), :]
            if c > 0:
                value += acc[pl.ds(h * TROWS + c + 3, LEVELS, stride=8), :]
            mom[c, 0:LEVELS, 128 * h : 128 * h + 128] = value
    for c in range(4):
        sz[c : c + 1, :] = mom[c, 32:33, :]
        sx[2 * c : 2 * c + 2, :] = mom[c, 33:35, :]
        sy[2 * c : 2 * c + 2, :] = mom[c, 35:37, :]
        se[c : c + 1, :] = mom[c, 37:38, :]

    def halo_copies(src, dst, ss, rs, sign):
        copies = []
        for i, (dx, dy, dz) in enumerate(HALO):
            s = src[min(i, 3)]
            t = dst[i] if i < 3 else dst[3].at[i - 3]
            copies.append(
                pltpu.make_async_remote_copy(
                    src_ref=s,
                    dst_ref=t,
                    send_sem=ss.at[i],
                    recv_sem=rs.at[i],
                    device_id=device(sign * dx, sign * dy, dz),
                    device_id_type=MESH,
                )
            )
        return copies

    halo = halo_copies((sx, sy, sz, se), (rx, ry, rz, re), halo_ss, halo_rs, 1)
    for copy in reversed(halo):
        copy.start()

    row32 = lax.broadcasted_iota(jnp.int32, (32, 256), 0)
    col32 = lax.broadcasted_iota(jnp.int32, (32, 256), 1)
    mask_face = (col32 % 16) == (row32 % 16)
    mask_edge = (
        ((col32 < 32) & (row32 == 0))
        | ((col32 >= 32) & (col32 < 64) & (col32 - 32 == row32))
        | ((col32 == 64) & (row32 == 0))
    )
    er = lax.broadcasted_iota(jnp.int32, (256, 256), 0)
    ec = lax.broadcasted_iota(jnp.int32, (256, 256), 1)

    def as_bf(mask):
        return jnp.where(mask, 1.0, 0.0).astype(BF)

    E_s[0:256, :] = as_bf(ec == er // 16)
    E_s[256:512, :] = as_bf(ec == (er // 16) * 16)
    target = jnp.where(er < 16, er, jnp.where(er < 32, (er - 16) * 16, 0))
    E_s[512:768, :] = as_bf(ec == target)
    bond_s[:, :, 0:BONDS] = bond_list[...]
    first = jnp.where(bond_live, bond_s[0], -1)
    second = jnp.where(bond_live, bond_s[1], -1)
    D_s[...] = (
        jnp.where(er == first, 1.0, 0.0) - jnp.where(er == second, 1.0, 0.0)
    ).astype(BF)

    row_c = lax.broadcasted_iota(jnp.int32, (72, 256), 0)
    block = row_c // 4
    comp = row_c % 4
    bx = block // 6 - 1
    by = (block // 2) % 3 - 1
    wrap_x = jnp.where(ix + bx < 0, -128.0, jnp.where(ix + bx > 7, 128.0, 0.0))
    wrap_y = jnp.where(iy + by < 0, -128.0, jnp.where(iy + by > 7, 128.0, 0.0))
    image = jnp.where(comp == 0, wrap_x, jnp.where(comp == 1, wrap_y, 0.0))
    wrapped = (comp == 2) & (block % 2 == 1)
    centre = anchor[2] + 16.0
    upper = ((comp == 0) & (bx == 1)) | ((comp == 1) & (by == 1))
    G_s[...] = jnp.zeros_like(G_s)

    def forces(exchange):
        own = slot(0, 0, 0)
        for k in range(18):
            if k == own:
                G_s[0:4, :] = psend[exchange]
                P_s[4 * k : 4 * k + 4, :] = psend[exchange]
            else:
                P_s[4 * k : 4 * k + 4, :] = ghost[exchange, k]
        GT_s[...] = G_s[...].T
        at = P_s[...] + image
        turns = jnp.floor((at - centre) * (1.0 / 64.0) + 0.5)
        at = jnp.where(wrapped, at - 64.0 * turns, at)
        at = jnp.where(upper & (at < -500.0), -3.0 * far_point, at)
        P_s[...] = at
        M_s[0:24, :] = 0.5 * (at[0:24] + at[48:72])
        M_s[24:32, :] = 0.5 * (at[24:32] + at[40:48])

        def group(j, carry):
            here = []
            for t in range(8):
                tile = GT_s[pl.ds(pl.multiple_of(64 * j + 8 * t, 8), 8), :]
                here.append([jnp.broadcast_to(tile[:, d : d + 1], (8, 128)) for d in range(3)])
            twice = [here[t][1] + here[t][1] for t in range(8)]
            sums = [jnp.zeros((8, 128), F32) for i in range(24)]

            def choose(mask, a, b):
                return [jnp.where(mask, a[d], b[d]) for d in range(3)]

            def add(t, other):
                differ = [here[t][d] - other[d] for d in range(3)]
                square = differ[0] * differ[0] + differ[1] * differ[1] + differ[2] * differ[2]
                inverse = 1.0 / jnp.where(square > 0.25, square, 1.0e6)
                sixth = inverse * inverse * inverse
                weight = jnp.maximum(48.0 * sixth - 24.0, 0.0) * sixth * inverse
                for d in range(3):
                    sums[3 * t + d] = sums[3 * t + d] + weight * differ[d]

            for h in range(2):
                half = slice(128 * h, 128 * h + 128)

                def row(ref, r):
                    return jnp.broadcast_to(ref[r : r + 1, half], (8, 128))

                def ghost_at(dx, dy, dz):
                    return [row(P_s, 4 * slot(dx, dy, dz) + d) for d in range(3)]

                for dz in (0, 1):
                    inner = ghost_at(0, 0, dz)
                    for t in range(8):
                        add(t, inner)
                    low, high = ghost_at(0, -1, dz), ghost_at(0, 1, dz)
                    half_way = row(M_s, 4 * slot(0, -1, dz) + 1)
                    for t in range(8):
                        add(t, choose(here[t][1] < half_way, low, high))
                    near = [[] for t in range(8)]
                    for dy in (0, -1, 1):
                        low, high = ghost_at(-1, dy, dz), ghost_at(1, dy, dz)
                        half_way = row(M_s, 4 * slot(-1, dy, dz))
                        for t in range(8):
                            near[t].append(choose(here[t][0] < half_way, low, high))
                    for t in range(8):
                        side, low, high = near[t]
                        add(t, side)
                        add(t, choose(twice[t] < low[1] + high[1], low, high))
            for t in range(8):
                for d in range(3):
                    A_s[pl.ds(pl.multiple_of(256 * d + 64 * j + 8 * t, 8), 8), :] = sums[3 * t + d]
            return carry

        lax.fori_loop(0, 4, group, 0)
        ones = jnp.ones((8, 128), BF)
        pieces = split3(A_s[...])
        pair = nt(ones, pieces[0]) + nt(ones, pieces[1]) + nt(ones, pieces[2])
        pieces = split3(jnp.concatenate([psend[exchange], psend[exchange]], 0))
        hot = D_s[...]
        differ = nn(pieces[0], hot) + nn(pieces[1], hot) + nn(pieces[2], hot)
        square = jnp.sum(jnp.where(sub256 < 3, differ * differ, 0.0), axis=0, keepdims=True)
        weight = jnp.where(bond_live, -spring / (1.0 - square / reach_square), 0.0)
        pieces = split3(weight * differ)
        pull = nt(pieces[0], hot) + nt(pieces[1], hot) + nt(pieces[2], hot)
        return [pair[0:1, 256 * d : 256 * d + 256] + pull[d : d + 1, :] for d in range(3)]

    sub256 = lax.broadcasted_iota(jnp.int32, (8, 256), 0)
    bead_arrive(0)
    push = forces(0)

    for copy in halo_copies((sx, sy, sz, se), (rx, ry, rz, re), halo_ss, halo_rs, -1):
        copy.wait_recv()
    zero_face = jnp.zeros((32, 256), F32)
    spread = []
    for c in range(4):
        edge = jnp.where(
            lane256 < 16,
            re[0, c : c + 1, :],
            jnp.where(
                lane256 < 32,
                re[1, c : c + 1, :],
                jnp.where(lane256 < 64, re[2, c : c + 1, :], re[3, c : c + 1, :]),
            ),
        )
        low_half = row32 < 16
        vx = jnp.where(low_half, rx[2 * c : 2 * c + 1, :], rx[2 * c + 1 : 2 * c + 2, :])
        vy = jnp.where(low_half, ry[2 * c : 2 * c + 1, :], ry[2 * c + 1 : 2 * c + 2, :])
        spread.append(
            jnp.concatenate(
                [
                    jnp.where(mask_face, vx, zero_face),
                    jnp.where(mask_face, vy, zero_face),
                    jnp.where(mask_edge, edge, zero_face),
                ],
                1,
            )
        )
    pieces = split3(jnp.concatenate(spread, 0))
    moved = nn(pieces[0], E_s[...]) + nn(pieces[1], E_s[...]) + nn(pieces[2], E_s[...])
    total = []
    for c in range(4):
        value = mom[c, 0:32, :] + moved[32 * c : 32 * c + 32, :]
        total.append(value + jnp.where(row32 == 0, rz[c : c + 1, :], 0.0))
    scale = 1.0 / jnp.maximum(total[0], 1.0)
    eye = (
        lax.broadcasted_iota(jnp.int32, (32, 32), 0) == lax.broadcasted_iota(jnp.int32, (32, 32), 1)
    )
    axis_here = nt(as_bf(eye), cell_axis[...].astype(F32).astype(BF))
    parts = [None] * 8
    for d in range(3):
        parts[d], parts[3 + d] = split2(total[1 + d] * scale)
    parts[6] = axis_here
    parts[7] = zero_face
    for c in range(8):
        for h in range(2):
            T_f[pl.ds(h * TROWS + c, 32, stride=8), :] = parts[c][:, 128 * h : 128 * h + 128]
    picked = nt(jnp.concatenate(parts[:7], 0).astype(BF), E_s[...])
    for q in range(4):
        if q < 3:
            value = picked[32 * q : 32 * q + 32, :] + picked[96 + 32 * q : 128 + 32 * q, :]
            uz[q : q + 1, :] = parts[q][0:1, :] + parts[3 + q][0:1, :]
        else:
            value = picked[192:224, :]
            uz[q : q + 1, :] = parts[6][0:1, :]
        vx = jnp.where(mask_face, value[:, 0:256], 0.0)
        vy = jnp.where(mask_face, value[:, 256:512], 0.0)
        ve = jnp.where(mask_edge, value[:, 512:768], 0.0)
        for j in range(2):
            half = slice(16 * j, 16 * j + 16)
            ux[2 * q + j : 2 * q + j + 1, :] = jnp.sum(vx[half], axis=0, keepdims=True)
            uy[2 * q + j : 2 * q + j + 1, :] = jnp.sum(vy[half], axis=0, keepdims=True)
        ue[q : q + 1, :] = jnp.sum(ve, axis=0, keepdims=True)
    info = halo_copies((ux, uy, uz, ue), (gx_, gy_, gz_, ge), info_ss, info_rs, -1)
    for copy in reversed(info):
        copy.start()
    for copy in halo_copies((ux, uy, uz, ue), (gx_, gy_, gz_, ge), info_ss, info_rs, 1):
        copy.wait_recv()

    def halo_level(level, channel, value):
        for h in range(2):
            row = h * TROWS + 8 * level + channel
            T_f[row : row + 1, :] = value[:, 128 * h : 128 * h + 128]

    for q in range(4):
        edge = jnp.where(
            lane256 < 16,
            ge[0, q : q + 1, :],
            jnp.where(
                lane256 < 32,
                ge[1, q : q + 1, :],
                jnp.where(lane256 < 64, ge[2, q : q + 1, :], ge[3, q : q + 1, :]),
            ),
        )
        edge = jnp.where(lane256 < 65, edge, 0.0)
        values = [gz_[q : q + 1, :]]
        values += [gx_[2 * q + j : 2 * q + j + 1, :] for j in range(2)]
        values += [gy_[2 * q + j : 2 * q + j + 1, :] for j in range(2)]
        values += [edge]
        for i, value in enumerate(values):
            if q < 3:
                high, low = split2(value)
                halo_level(32 + i, q, high)
                halo_level(32 + i, 3 + q, low)
            else:
                halo_level(32 + i, 6, value)
                halo_level(32 + i, 7, jnp.zeros((1, 256), F32))
    for h in range(2):
        half = slice(128 * h, 128 * h + 128)
        T_s[:, half] = T_f[h * TROWS : h * TROWS + TROWS, :].astype(BF)

    def look_rows(row0, count):
        hot = jnp.concatenate([hot_lo(row0 + r) for r in range(count)], 1)
        found = nn(T_s[...], hot)
        for r in range(count):
            row = row0 + r
            level = rows_of(hi_s, row, 8).astype(jnp.int32)
            values = [
                found[8 * j : 8 * j + 8, 128 * r : 128 * r + 128] for j in range(LEVELS)
            ]
            bit = 1
            while len(values) > 1:
                odd = (level & bit) != 0
                values = [
                    jnp.where(odd, values[i + 1], values[i]) if i + 1 < len(values) else values[i]
                    for i in range(0, len(values), 2)
                ]
                bit = 2 * bit
            V_s[pl.ds(pl.multiple_of(row * 8, 8), 8), :] = values[0]

    def collide(row0, v):
        read = [V_s[pl.ds(row0 * 8 + c, 8, stride=8), :] for c in range(7)]
        u = [read[d] + read[3 + d] for d in range(3)]
        index = read[6].astype(jnp.int32)
        n = [
            jnp.take_along_axis(axis_tab[8 * d : 8 * d + 8, :], index, axis=1) for d in range(3)
        ]
        return rotated(v, u, n)

    def emit(row0, p, v, live):
        new = collide(row0, v)
        for d in range(3):
            offset = p[d] - jnp.floor(p[d]) - 0.5
            vel_out[d, pl.ds(row0, 8), :] = new[d]
            off_out[d, pl.ds(row0, 8), :] = jnp.where(live, offset, 2.0)

    def emit_step(b):
        for i in range(STEP // 8):
            emit(*solvent(b, i))

    def look_loop(b, carry):
        emit_step(jnp.maximum(b - 1, 0))
        look_rows(pl.multiple_of(b * STEP, 8), STEP)
        return carry

    look_rows(SOLV, 2)
    new = collide(SOLV, [bpack[3 + d] for d in range(3)])
    speed = []
    for d in range(3):
        W_s[d] = new[d]
        speed.append(jnp.concatenate([W_s[d, 0:1, :], W_s[d, 1:2, :]], 1))

    def out_copies(part):
        rows = pl.ds(part * HALF, HALF) if part < 2 else pl.ds(RES, SOLV - RES)
        return [
            pltpu.make_async_copy(
                off_out.at[:, rows], off_hbm.at[:, rows], out_sem.at[0, part]
            ),
            pltpu.make_async_copy(
                vel_out.at[:, rows], vel_hbm.at[:, rows], out_sem.at[1, part]
            ),
        ]

    half_kick = 0.5 * step_size / bead_mass

    def substep(t, carry):
        speed, gone, push = carry[0:3], carry[3:6], carry[6:9]
        speed = [speed[d] + half_kick * push[d] for d in range(3)]
        gone = [gone[d] + step_size * speed[d] for d in range(3)]
        place(t + 1, [start[d] + gone[d] for d in range(3)])
        bead_send(t + 1)
        lax.fori_loop(
            HSTEPS * t, jnp.minimum(HSTEPS * (t + 1), STEPS), look_loop, 0
        )

        @pl.when(t == 1)
        def _():
            for copy in out_copies(0):
                copy.start()

        @pl.when(t == 2)
        def _():
            emit_step(STEPS - 1)
            for part in (1, 2):
                for copy in out_copies(part):
                    copy.start()

        bead_arrive(t + 1)
        push = forces(t + 1)
        speed = [speed[d] + half_kick * push[d] for d in range(3)]
        return (*speed, *gone, *push)

    still = jnp.zeros((1, 256), F32)
    last = lax.fori_loop(0, 3, substep, (*speed, still, still, still, *push))
    for d in range(3):
        bpos_out[d] = last[3 + d]
        bvel_out[d] = last[d]
    for part in range(3):
        for copy in out_copies(part):
            copy.wait()

    for g in range(6):
        for copy in mig_copies(g, g ^ 1):
            copy.wait_send()
    for copy in halo:
        copy.wait_send()
    for copy in info:
        copy.wait_send()
    for exchange in range(4):
        for dx, dy, dz in OFFSETS:
            bead_copy(exchange, (dx, dy, dz), slot(-dx, -dy, dz)).wait_send()


def shards(
    sol_pos,
    sol_vel,
    sol_rows,
    mig_pos,
    mig_vel,
    mig_rows,
    bead_pos,
    bead_vel,
    bead_chains,
    bond_list,
    cell_axis,
    shift,
):
    vmem = pl.BlockSpec(memory_space=pltpu.VMEM)
    smem = pl.BlockSpec(memory_space=pltpu.SMEM)
    anywhere = pl.BlockSpec(memory_space=pl.ANY)
    dma = pltpu.SemaphoreType.DMA
    f32 = lambda *shape: pltpu.VMEM(shape, F32)
    bf = lambda *shape: pltpu.VMEM(shape, BF)
    outs = pl.pallas_call(
        kernel,
        out_shape=(
            jax.ShapeDtypeStruct((3, SOLV, 128), F32),
            jax.ShapeDtypeStruct((3, SOLV, 128), F32),
            jax.ShapeDtypeStruct((3, 1, BEADS), F32),
            jax.ShapeDtypeStruct((3, 1, BEADS), F32),
        ),
        in_specs=[smem] * 4 + [anywhere] * 4 + [vmem] * 5,
        out_specs=(anywhere, anywhere, vmem, vmem),
        scratch_shapes=[
            f32(3, SOLV, 128),
            f32(3, SOLV, 128),
            f32(3, SOLV, 128),
            f32(3, SOLV, 128),
            pltpu.VMEM((2, 1, 256), jnp.int32),
            f32(ALL, 128),
            f32(ALL, 128),
            f32(ALL * 8, 128),
            f32(2 * TROWS, 128),
            bf(256, 128),
            bf(TROWS, 128),
            pltpu.VMEM((72, 128), jnp.int32),
            pltpu.VMEM((6, 1, 128), jnp.int32),
            pltpu.VMEM((6, 1, 128), jnp.int32),
            f32(6, 8, 128),
            f32(4, 40, 256),
            bf(768, 256),
            bf(256, 256),
            f32(8, 256),
            f32(8, 256),
            f32(4, 256),
            f32(4, 256),
            f32(8, 256),
            f32(8, 256),
            f32(4, 256),
            f32(4, 4, 256),
            f32(8, 256),
            f32(8, 256),
            f32(4, 256),
            f32(4, 256),
            f32(8, 256),
            f32(8, 256),
            f32(4, 256),
            f32(4, 4, 256),
            f32(4, 32, 256),
            f32(2 * TROWS, 128),
            bf(TROWS, 256),
            f32(4, 4, 256),
            f32(4, 18, 4, 256),
            f32(128, 256),
            f32(256, 128),
            f32(72, 256),
            f32(32, 256),
            f32(768, 128),
            f32(3, 8, 128),
            dma((3, 6)),
            dma((3, 6)),
            dma((7,)),
            dma((7,)),
            dma((7,)),
            dma((7,)),
            dma((4, 18)),
            dma((4, 18)),
            dma((2, 2)),
            dma((2, 3)),
            pltpu.SemaphoreType.REGULAR((2,)),
        ],
        compiler_params=pltpu.CompilerParams(
            collective_id=0, has_side_effects=True, vmem_limit_bytes=60 * 1024 * 1024
        ),
        name="interval",
    )(
        sol_rows.reshape(1),
        mig_rows.reshape(6),
        bead_chains.reshape(1),
        shift,
        sol_pos.reshape(3, RES, 128),
        sol_vel.reshape(3, RES, 128),
        mig_pos.reshape(3, 6, FACE, 128),
        mig_vel.reshape(3, 6, FACE, 128),
        bead_pos.reshape(3, 1, BEADS),
        bead_vel.reshape(3, 1, BEADS),
        bond_list.reshape(2, 1, BONDS),
        cell_axis.reshape(256, 32),
        jnp.asarray(axis_rows()),
    )
    offset, vel, bpos, bvel = outs
    live = offset < 1.0
    bead_live = jnp.arange(BEADS, dtype=jnp.int32) < CHAIN * bead_chains.reshape(())
    return (
        jnp.where(live, offset + 3.0 * step_size * vel, 0.0).reshape(3, 1, 1, 1, SOLV * 128),
        jnp.where(live, vel, 0.0).reshape(3, 1, 1, 1, SOLV * 128),
        jnp.where(bead_live, bpos, 0.0).reshape(3, 1, 1, 1, BEADS),
        jnp.where(bead_live, bvel, 0.0).reshape(3, 1, 1, 1, BEADS),
    )


def solution(mesh):
    return jax.shard_map(
        shards,
        mesh=mesh,
        in_specs=(
            P(None, "gx", "gy", "gz", None),
            P(None, "gx", "gy", "gz", None),
            P("gx", "gy", "gz"),
            P(None, "gx", "gy", "gz", None, None),
            P(None, "gx", "gy", "gz", None, None),
            P("gx", "gy", "gz", None),
            P(None, "gx", "gy", "gz", None),
            P(None, "gx", "gy", "gz", None),
            P("gx", "gy", "gz"),
            P(None, "gx", "gy", "gz", None),
            P("gx", "gy", "gz"),
            P(),
        ),
        out_specs=(
            P(None, "gx", "gy", "gz", None),
            P(None, "gx", "gy", "gz", None),
            P(None, "gx", "gy", "gz", None),
            P(None, "gx", "gy", "gz", None),
        ),
        check_vma=False,
    )
```

```python
import math

import jax
import jax.numpy as jnp
import numpy as np
from jax import lax
from jax.experimental import pallas as pl
from jax.experimental.pallas import tpu as pltpu
from jax.sharding import PartitionSpec as P

BF = jnp.bfloat16
F32 = jnp.float32
MESH = pl.DeviceIdType.MESH

UNITS = 16
NAXES = 32
CHAIN = 8
bead_mass = 5.0
step_size = 0.02
spring = 30.0
reach_square = 2.25
far_point = -1000.0
cut_square = 2.0 ** (1.0 / 3.0)
turn_cosine = math.cos(130.0 * math.pi / 180.0)
turn_sine = math.sin(130.0 * math.pi / 180.0)
golden = math.pi * (3.0 - math.sqrt(5.0))

LANES = 256
LEVELS = 38
CH = 8
TROWS = LEVELS * CH
RES = 384
FACE = 24
SOLV = RES + 6 * FACE
ALL = SOLV + 8
STEP = 2 * FACE
BEADS = 256
BONDS = 224

OFFSETS = [
    (dx, dy, dz)
    for dx in (-1, 0, 1)
    for dy in (-1, 0, 1)
    for dz in (0, 1)
    if (dx, dy, dz) != (0, 0, 0)
]
OFFSETS.sort(key=lambda off: -(abs(off[0]) + abs(off[1]) + 2 * off[2]))
FACES = [(-1, 0, 0), (1, 0, 0), (0, -1, 0), (0, 1, 0), (0, 0, 1)]
HALO = [(1, 0, 0), (0, 1, 0), (0, 0, 1), (1, 0, 1), (0, 1, 1), (1, 1, 0), (1, 1, 1)]


def slot(dx, dy, dz):
    return ((dx + 1) * 3 + dy + 1) * 2 + dz


def axis_rows():
    counter = np.arange(128) % NAXES
    height = 1.0 - (2.0 * counter + 1.0) / NAXES
    radius = np.sqrt(1.0 - height * height)
    rows = np.stack(
        [radius * np.cos(golden * counter), radius * np.sin(golden * counter), height]
    )
    return np.repeat(rows, 8, axis=0).astype(np.float32)


def split2(value):
    high = value.astype(BF).astype(F32)
    return high, (value - high).astype(BF).astype(F32)


def split3(value):
    high = value.astype(BF)
    rest = value - high.astype(F32)
    middle = rest.astype(BF)
    low = (rest - middle.astype(F32)).astype(BF)
    return high, middle, low


def nt(a, b):
    return lax.dot_general(a, b, (((1,), (1,)), ((), ())), preferred_element_type=F32)


def nn(a, b):
    return lax.dot_general(a, b, (((1,), (0,)), ((), ())), preferred_element_type=F32)


def rows_of(ref, row, count):
    return jnp.broadcast_to(ref[pl.ds(row, 1), :], (count, 128))


def rotated(v, u, n):
    w = [v[d] - u[d] for d in range(3)]
    along = (1.0 - turn_cosine) * (n[0] * w[0] + n[1] * w[1] + n[2] * w[2])
    crossed = [
        n[1] * w[2] - n[2] * w[1],
        n[2] * w[0] - n[0] * w[2],
        n[0] * w[1] - n[1] * w[0],
    ]
    return [u[d] + turn_cosine * w[d] + turn_sine * crossed[d] + along * n[d] for d in range(3)]


def kernel(
    sol_rows,
    mig_rows,
    chains,
    shift,
    sol_pos_hbm,
    sol_vel_hbm,
    mig_pos,
    mig_vel,
    bead_pos,
    bead_vel,
    bond_list,
    cell_axis,
    axis_tab,
    off_hbm,
    vel_hbm,
    bpos_out,
    bvel_out,
    sol_pos,
    sol_vel,
    off_out,
    vel_out,
    bond_s,
    lo_s,
    hi_s,
    V_s,
    acc,
    iota_lo,
    iota_hi,
    limit,
    arr_rows,
    row_send,
    bpack,
    mom,
    E_s,
    D_s,
    sx,
    sy,
    sz,
    se,
    rx,
    ry,
    rz,
    re,
    ux,
    uy,
    uz,
    ue,
    gx_,
    gy_,
    gz_,
    ge,
    U_s,
    T_f,
    T_s,
    psend,
    ghost,
    G_s,
    GT_s,
    P_s,
    M_s,
    A_s,
    W_s,
    mig_ss,
    mig_rs,
    halo_ss,
    halo_rs,
    info_ss,
    info_rs,
    bead_ss,
    bead_rs,
    in_sem,
    out_sem,
    entered,
):
    ix = lax.axis_index("gx")
    iy = lax.axis_index("gy")
    iz = lax.axis_index("gz")

    def device(dx, dy, dz):
        return (
            lax.rem(ix + dx + 8, 8),
            lax.rem(iy + dy + 8, 8),
            lax.rem(iz + dz + 2, 2),
        )

    barrier = pltpu.get_barrier_semaphore()

    def tell(sem):
        for off in FACES:
            pl.semaphore_signal(sem, inc=1, device_id=device(*off), device_id_type=MESH)

    tell(barrier)

    HALF = RES // 2

    def in_copies(chunk):
        part = pl.ds(chunk * HALF, HALF)
        return [
            pltpu.make_async_copy(
                sol_pos_hbm.at[:, part], sol_pos.at[:, part], in_sem.at[0, chunk]
            ),
            pltpu.make_async_copy(
                sol_vel_hbm.at[:, part], sol_vel.at[:, part], in_sem.at[1, chunk]
            ),
        ]

    for chunk in range(2):
        for copy in in_copies(chunk):
            copy.start()

    iota_lo[...] = lax.broadcasted_iota(jnp.int32, (256, 128), 0).astype(F32).astype(BF)
    iota_hi[...] = (
        (lax.broadcasted_iota(jnp.int32, (TROWS, 128), 0) // CH).astype(F32).astype(BF)
    )
    acc[...] = jnp.zeros_like(acc)
    bpack[...] = jnp.zeros_like(bpack)
    one16 = jnp.ones((16, 128), BF)
    zero16 = jnp.zeros((16, 128), BF)
    sub8 = lax.broadcasted_iota(jnp.int32, (8, 128), 0)
    lane256 = lax.broadcasted_iota(jnp.int32, (1, 256), 1)
    anchor = [(ix * 16).astype(F32), (iy * 16).astype(F32), (iz * 32).astype(F32)]
    shifts = [shift[d].astype(F32) for d in range(3)]
    bead_live = lane256 < CHAIN * chains[0]
    bond_live = lane256 < (CHAIN - 1) * chains[0]

    start = [bead_pos[d] for d in range(3)]

    def place(exchange, value):
        for d in range(3):
            psend[exchange, d : d + 1, :] = jnp.where(bead_live, value[d], far_point)
        psend[exchange, 3:4, :] = jnp.zeros((1, 256), F32)

    place(0, start)
    for g in range(6):
        row_send[g] = jnp.broadcast_to(mig_rows[g], (1, 128)).astype(jnp.int32)

    def prep(row0, p, v, weight):
        level = []
        for d in range(3):
            level.append(jnp.floor((p[d] * 16.0 + shifts[d]) * 0.0625) - anchor[d])
        lx, ly, lz = level
        xe = lx > 15.5
        ye = ly > 15.5
        ze = lz > 31.5
        zb = jnp.where(lz > 15.5, 1.0, 0.0)
        zm = lz - 16.0 * zb
        both = xe & ye
        edge = xe | ye
        along = jnp.where(xe, ly, lx)
        lo_edge = jnp.where(
            both,
            32.0 + lz,
            jnp.where(ze, along + jnp.where(xe, 0.0, 16.0), along * 16.0 + zm),
        )
        hi_edge = jnp.where(both | ze, 37.0, jnp.where(xe, 33.0, 35.0) + zb)
        lo_s[pl.ds(row0, 8), :] = jnp.where(edge, lo_edge, lx * 16.0 + ly)
        hi_s[pl.ds(row0, 8), :] = jnp.where(edge, hi_edge, lz)
        V_s[pl.ds(row0 * 8, 8, stride=8), :] = weight
        for d in range(3):
            high, low = split2(weight * v[d])
            V_s[pl.ds(row0 * 8 + 1 + d, 8, stride=8), :] = high
            V_s[pl.ds(row0 * 8 + 4 + d, 8, stride=8), :] = low
        V_s[pl.ds(row0 * 8 + 7, 8, stride=8), :] = jnp.zeros((8, 128), F32)

    limit[0 : RES // 8, :] = jnp.broadcast_to(sol_rows[0], (RES // 8, 128)).astype(jnp.int32)

    def solvent(b, i):
        r = pl.multiple_of(b * STEP + 8 * i, 8)
        live = sub8 + r < limit[pl.ds(b * (STEP // 8) + i, 1), :]
        return (
            r,
            [sol_pos[d, pl.ds(r, 8), :] for d in range(3)],
            [sol_vel[d, pl.ds(r, 8), :] for d in range(3)],
            live,
        )

    def prep_step(b):
        for i in range(STEP // 8):
            r, p, v, live = solvent(b, i)
            prep(r, p, v, jnp.where(live, 1.0, 0.0))

    faces = [(-1, 0, 0), (1, 0, 0), (0, -1, 0), (0, 1, 0), (0, 0, 1), (0, 0, 1)]

    def mig_copies(g, f):
        where = dict(device_id=device(*faces[g]), device_id_type=MESH)
        return [
            pltpu.make_async_remote_copy(
                src_ref=mig_pos.at[:, g],
                dst_ref=sol_pos.at[:, pl.ds(RES + FACE * f, FACE)],
                send_sem=mig_ss.at[0, g],
                recv_sem=mig_rs.at[0, f],
                **where,
            ),
            pltpu.make_async_remote_copy(
                src_ref=mig_vel.at[:, g],
                dst_ref=sol_vel.at[:, pl.ds(RES + FACE * f, FACE)],
                send_sem=mig_ss.at[1, g],
                recv_sem=mig_rs.at[1, f],
                **where,
            ),
            pltpu.make_async_remote_copy(
                src_ref=row_send.at[g],
                dst_ref=arr_rows.at[f],
                send_sem=mig_ss.at[2, g],
                recv_sem=mig_rs.at[2, f],
                **where,
            ),
        ]

    def bead_copy(exchange, off, into):
        return pltpu.make_async_remote_copy(
            src_ref=psend.at[exchange],
            dst_ref=ghost.at[exchange, into],
            send_sem=bead_ss.at[exchange, slot(*off)],
            recv_sem=bead_rs.at[exchange, into],
            device_id=device(*off),
            device_id_type=MESH,
        )

    def bead_send(exchange):
        for dx, dy, dz in OFFSETS:
            bead_copy(exchange, (dx, dy, dz), slot(-dx, -dy, dz)).start()

    def bead_arrive(exchange):
        for off in OFFSETS:
            bead_copy(exchange, off, slot(*off)).wait_recv()

    def hot_lo(row):
        lo_b = rows_of(lo_s, row, 16).astype(BF)
        return jnp.concatenate(
            [
                jnp.where(iota_lo[16 * j : 16 * j + 16, :] == lo_b, one16, zero16)
                for j in range(16)
            ],
            0,
        )

    def bin_rows(row0, count):
        spread = []
        hot = []
        for r in range(count):
            row = row0 + r
            hot.append(hot_lo(row))
            v = V_s[pl.ds(pl.multiple_of(row * 8, 8), 8), :]
            v = jnp.concatenate([v, v], 0).astype(BF)
            hi_b = rows_of(hi_s, row, 16).astype(BF)
            spread.append(
                jnp.concatenate(
                    [
                        jnp.where(iota_hi[16 * j : 16 * j + 16, :] == hi_b, v, zero16)
                        for j in range(TROWS // 16)
                    ],
                    0,
                )
            )
        sums = nt(jnp.concatenate(spread, 1), jnp.concatenate(hot, 1))
        acc[0:TROWS, :] += sums[:, 0:128]
        acc[TROWS : 2 * TROWS, :] += sums[:, 128:256]

    for d in range(3):
        for h in range(2):
            half = slice(128 * h, 128 * h + 128)
            bpack[d, h : h + 1, :] = start[d][:, half]
            bpack[3 + d, h : h + 1, :] = bead_vel[d][:, half]
    lane8 = lax.broadcasted_iota(jnp.int32, (8, 128), 1) + 128 * sub8
    bead_here = (lane8 < CHAIN * chains[0]) & (sub8 < 2)
    prep(
        SOLV,
        [bpack[d] for d in range(3)],
        [bpack[3 + d] for d in range(3)],
        jnp.where(bead_here, bead_mass, 0.0),
    )
    bin_rows(SOLV, 2)
    RSTEPS = RES // STEP
    HSTEPS = RSTEPS // 2

    STEPS = SOLV // STEP
    for copy in in_copies(0):
        copy.wait()
    prep_step(0)

    def bin_loop(b, carry):
        @pl.when(b == 2)
        def _():
            pl.semaphore_wait(barrier, len(FACES))
            for g in (4, 5, 0, 1, 2, 3):
                for copy in mig_copies(g, g ^ 1):
                    copy.start()
            tell(entered.at[0])

        @pl.when(b == HSTEPS - 1)
        def _():
            for copy in in_copies(1):
                copy.wait()

        @pl.when(b == HSTEPS)
        def _():
            pl.semaphore_wait(entered.at[0], len(FACES))
            tell(entered.at[1])

        @pl.when(b == HSTEPS + 2)
        def _():
            pl.semaphore_wait(entered.at[1], len(FACES))
            bead_send(0)

        for pair in range(3):

            @pl.when(b == RSTEPS - 1 + pair)
            def _():
                for f in (2 * pair, 2 * pair + 1):
                    for copy in mig_copies(f, f):
                        copy.wait_recv()
                    first = (RES + FACE * f) // 8
                    limit[first : first + FACE // 8, :] = (
                        jnp.broadcast_to(arr_rows[f], (FACE // 8, 128)) + RES + FACE * f
                    )

        bin_rows(pl.multiple_of(b * STEP, 8), STEP)
        prep_step(jnp.minimum(b + 1, STEPS - 1))
        return carry

    lax.fori_loop(0, STEPS, bin_loop, 0)

    for c in range(4):
        for h in range(2):
            value = acc[pl.ds(h * TROWS + c, LEVELS, stride=8), :]
            if c > 0:
                value += acc[pl.ds(h * TROWS + c + 3, LEVELS, stride=8), :]
            mom[c, 0:LEVELS, 128 * h : 128 * h + 128] = value
    for c in range(4):
        sz[c : c + 1, :] = mom[c, 32:33, :]
        sx[2 * c : 2 * c + 2, :] = mom[c, 33:35, :]
        sy[2 * c : 2 * c + 2, :] = mom[c, 35:37, :]
        se[c : c + 1, :] = mom[c, 37:38, :]

    def halo_copies(src, dst, ss, rs, sign):
        copies = []
        for i, (dx, dy, dz) in enumerate(HALO):
            s = src[min(i, 3)]
            t = dst[i] if i < 3 else dst[3].at[i - 3]
            copies.append(
                pltpu.make_async_remote_copy(
                    src_ref=s,
                    dst_ref=t,
                    send_sem=ss.at[i],
                    recv_sem=rs.at[i],
                    device_id=device(sign * dx, sign * dy, dz),
                    device_id_type=MESH,
                )
            )
        return copies

    halo = halo_copies((sx, sy, sz, se), (rx, ry, rz, re), halo_ss, halo_rs, 1)
    for copy in reversed(halo):
        copy.start()

    row32 = lax.broadcasted_iota(jnp.int32, (32, 256), 0)
    col32 = lax.broadcasted_iota(jnp.int32, (32, 256), 1)
    mask_face = (col32 % 16) == (row32 % 16)
    mask_edge = (
        ((col32 < 32) & (row32 == 0))
        | ((col32 >= 32) & (col32 < 64) & (col32 - 32 == row32))
        | ((col32 == 64) & (row32 == 0))
    )
    er = lax.broadcasted_iota(jnp.int32, (256, 256), 0)
    ec = lax.broadcasted_iota(jnp.int32, (256, 256), 1)

    def as_bf(mask):
        return jnp.where(mask, 1.0, 0.0).astype(BF)

    E_s[0:256, :] = as_bf(ec == er // 16)
    E_s[256:512, :] = as_bf(ec == (er // 16) * 16)
    target = jnp.where(er < 16, er, jnp.where(er < 32, (er - 16) * 16, 0))
    E_s[512:768, :] = as_bf(ec == target)
    bond_s[:, :, 0:BONDS] = bond_list[...]
    first = jnp.where(bond_live, bond_s[0], -1)
    second = jnp.where(bond_live, bond_s[1], -1)
    D_s[...] = (
        jnp.where(er == first, 1.0, 0.0) - jnp.where(er == second, 1.0, 0.0)
    ).astype(BF)

    row_c = lax.broadcasted_iota(jnp.int32, (72, 256), 0)
    block = row_c // 4
    comp = row_c % 4
    bx = block // 6 - 1
    by = (block // 2) % 3 - 1
    wrap_x = jnp.where(ix + bx < 0, -128.0, jnp.where(ix + bx > 7, 128.0, 0.0))
    wrap_y = jnp.where(iy + by < 0, -128.0, jnp.where(iy + by > 7, 128.0, 0.0))
    image = jnp.where(comp == 0, wrap_x, jnp.where(comp == 1, wrap_y, 0.0))
    wrapped = (comp == 2) & (block % 2 == 1)
    centre = anchor[2] + 16.0
    upper = ((comp == 0) & (bx == 1)) | ((comp == 1) & (by == 1))
    G_s[...] = jnp.zeros_like(G_s)

    def forces(exchange):
        own = slot(0, 0, 0)
        for k in range(18):
            if k == own:
                G_s[0:4, :] = psend[exchange]
                P_s[4 * k : 4 * k + 4, :] = psend[exchange]
            else:
                P_s[4 * k : 4 * k + 4, :] = ghost[exchange, k]
        GT_s[...] = G_s[...].T
        at = P_s[...] + image
        turns = jnp.floor((at - centre) * (1.0 / 64.0) + 0.5)
        at = jnp.where(wrapped, at - 64.0 * turns, at)
        at = jnp.where(upper & (at < -500.0), -3.0 * far_point, at)
        P_s[...] = at
        M_s[0:24, :] = 0.5 * (at[0:24] + at[48:72])
        M_s[24:32, :] = 0.5 * (at[24:32] + at[40:48])

        def group(j, carry):
            here = []
            for t in range(8):
                tile = GT_s[pl.ds(pl.multiple_of(64 * j + 8 * t, 8), 8), :]
                here.append([jnp.broadcast_to(tile[:, d : d + 1], (8, 128)) for d in range(3)])
            twice = [here[t][1] + here[t][1] for t in range(8)]
            sums = [jnp.zeros((8, 128), F32) for i in range(24)]

            def choose(mask, a, b):
                return [jnp.where(mask, a[d], b[d]) for d in range(3)]

            def add(t, other):
                differ = [here[t][d] - other[d] for d in range(3)]
                square = differ[0] * differ[0] + differ[1] * differ[1] + differ[2] * differ[2]
                inverse = 1.0 / jnp.where(square > 0.25, square, 1.0e6)
                sixth = inverse * inverse * inverse
                weight = jnp.maximum(48.0 * sixth - 24.0, 0.0) * sixth * inverse
                for d in range(3):
                    sums[3 * t + d] = sums[3 * t + d] + weight * differ[d]

            for h in range(2):
                half = slice(128 * h, 128 * h + 128)

                def row(ref, r):
                    return jnp.broadcast_to(ref[r : r + 1, half], (8, 128))

                def ghost_at(dx, dy, dz):
                    return [row(P_s, 4 * slot(dx, dy, dz) + d) for d in range(3)]

                for dz in (0, 1):
                    inner = ghost_at(0, 0, dz)
                    for t in range(8):
                        add(t, inner)
                    low, high = ghost_at(0, -1, dz), ghost_at(0, 1, dz)
                    half_way = row(M_s, 4 * slot(0, -1, dz) + 1)
                    for t in range(8):
                        add(t, choose(here[t][1] < half_way, low, high))
                    near = [[] for t in range(8)]
                    for dy in (0, -1, 1):
                        low, high = ghost_at(-1, dy, dz), ghost_at(1, dy, dz)
                        half_way = row(M_s, 4 * slot(-1, dy, dz))
                        for t in range(8):
                            near[t].append(choose(here[t][0] < half_way, low, high))
                    for t in range(8):
                        side, low, high = near[t]
                        add(t, side)
                        add(t, choose(twice[t] < low[1] + high[1], low, high))
            for t in range(8):
                for d in range(3):
                    A_s[pl.ds(pl.multiple_of(256 * d + 64 * j + 8 * t, 8), 8), :] = sums[3 * t + d]
            return carry

        lax.fori_loop(0, 4, group, 0)
        ones = jnp.ones((8, 128), BF)
        pieces = split3(A_s[...])
        pair = nt(ones, pieces[0]) + nt(ones, pieces[1]) + nt(ones, pieces[2])
        pieces = split3(jnp.concatenate([psend[exchange], psend[exchange]], 0))
        hot = D_s[...]
        differ = nn(pieces[0], hot) + nn(pieces[1], hot) + nn(pieces[2], hot)
        square = jnp.sum(jnp.where(sub256 < 3, differ * differ, 0.0), axis=0, keepdims=True)
        weight = jnp.where(bond_live, -spring / (1.0 - square / reach_square), 0.0)
        pieces = split3(weight * differ)
        pull = nt(pieces[0], hot) + nt(pieces[1], hot) + nt(pieces[2], hot)
        return [pair[0:1, 256 * d : 256 * d + 256] + pull[d : d + 1, :] for d in range(3)]

    sub256 = lax.broadcasted_iota(jnp.int32, (8, 256), 0)
    bead_arrive(0)
    push = forces(0)

    for copy in halo_copies((sx, sy, sz, se), (rx, ry, rz, re), halo_ss, halo_rs, -1):
        copy.wait_recv()
    zero_face = jnp.zeros((32, 256), F32)
    spread = []
    for c in range(4):
        edge = jnp.where(
            lane256 < 16,
            re[0, c : c + 1, :],
            jnp.where(
                lane256 < 32,
                re[1, c : c + 1, :],
                jnp.where(lane256 < 64, re[2, c : c + 1, :], re[3, c : c + 1, :]),
            ),
        )
        low_half = row32 < 16
        vx = jnp.where(low_half, rx[2 * c : 2 * c + 1, :], rx[2 * c + 1 : 2 * c + 2, :])
        vy = jnp.where(low_half, ry[2 * c : 2 * c + 1, :], ry[2 * c + 1 : 2 * c + 2, :])
        spread.append(
            jnp.concatenate(
                [
                    jnp.where(mask_face, vx, zero_face),
                    jnp.where(mask_face, vy, zero_face),
                    jnp.where(mask_edge, edge, zero_face),
                ],
                1,
            )
        )
    pieces = split3(jnp.concatenate(spread, 0))
    moved = nn(pieces[0], E_s[...]) + nn(pieces[1], E_s[...]) + nn(pieces[2], E_s[...])
    total = []
    for c in range(4):
        value = mom[c, 0:32, :] + moved[32 * c : 32 * c + 32, :]
        total.append(value + jnp.where(row32 == 0, rz[c : c + 1, :], 0.0))
    scale = 1.0 / jnp.maximum(total[0], 1.0)
    eye = (
        lax.broadcasted_iota(jnp.int32, (32, 32), 0) == lax.broadcasted_iota(jnp.int32, (32, 32), 1)
    )
    axis_here = nt(as_bf(eye), cell_axis[...].astype(F32).astype(BF))
    parts = [None] * 8
    for d in range(3):
        parts[d], parts[3 + d] = split2(total[1 + d] * scale)
    parts[6] = axis_here
    parts[7] = zero_face
    for c in range(8):
        for h in range(2):
            T_f[pl.ds(h * TROWS + c, 32, stride=8), :] = parts[c][:, 128 * h : 128 * h + 128]
    picked = nt(jnp.concatenate(parts[:7], 0).astype(BF), E_s[...])
    for q in range(4):
        if q < 3:
            value = picked[32 * q : 32 * q + 32, :] + picked[96 + 32 * q : 128 + 32 * q, :]
            uz[q : q + 1, :] = parts[q][0:1, :] + parts[3 + q][0:1, :]
        else:
            value = picked[192:224, :]
            uz[q : q + 1, :] = parts[6][0:1, :]
        vx = jnp.where(mask_face, value[:, 0:256], 0.0)
        vy = jnp.where(mask_face, value[:, 256:512], 0.0)
        ve = jnp.where(mask_edge, value[:, 512:768], 0.0)
        for j in range(2):
            half = slice(16 * j, 16 * j + 16)
            ux[2 * q + j : 2 * q + j + 1, :] = jnp.sum(vx[half], axis=0, keepdims=True)
            uy[2 * q + j : 2 * q + j + 1, :] = jnp.sum(vy[half], axis=0, keepdims=True)
        ue[q : q + 1, :] = jnp.sum(ve, axis=0, keepdims=True)
    info = halo_copies((ux, uy, uz, ue), (gx_, gy_, gz_, ge), info_ss, info_rs, -1)
    for copy in reversed(info):
        copy.start()
    for copy in halo_copies((ux, uy, uz, ue), (gx_, gy_, gz_, ge), info_ss, info_rs, 1):
        copy.wait_recv()

    def halo_level(level, channel, value):
        for h in range(2):
            row = h * TROWS + 8 * level + channel
            T_f[row : row + 1, :] = value[:, 128 * h : 128 * h + 128]

    for q in range(4):
        edge = jnp.where(
            lane256 < 16,
            ge[0, q : q + 1, :],
            jnp.where(
                lane256 < 32,
                ge[1, q : q + 1, :],
                jnp.where(lane256 < 64, ge[2, q : q + 1, :], ge[3, q : q + 1, :]),
            ),
        )
        edge = jnp.where(lane256 < 65, edge, 0.0)
        values = [gz_[q : q + 1, :]]
        values += [gx_[2 * q + j : 2 * q + j + 1, :] for j in range(2)]
        values += [gy_[2 * q + j : 2 * q + j + 1, :] for j in range(2)]
        values += [edge]
        for i, value in enumerate(values):
            if q < 3:
                high, low = split2(value)
                halo_level(32 + i, q, high)
                halo_level(32 + i, 3 + q, low)
            else:
                halo_level(32 + i, 6, value)
                halo_level(32 + i, 7, jnp.zeros((1, 256), F32))
    for h in range(2):
        half = slice(128 * h, 128 * h + 128)
        T_s[:, half] = T_f[h * TROWS : h * TROWS + TROWS, :].astype(BF)

    def look_rows(row0, count):
        hot = jnp.concatenate([hot_lo(row0 + r) for r in range(count)], 1)
        found = nn(T_s[...], hot)
        for r in range(count):
            row = row0 + r
            level = rows_of(hi_s, row, 8).astype(jnp.int32)
            values = [
                found[8 * j : 8 * j + 8, 128 * r : 128 * r + 128] for j in range(LEVELS)
            ]
            bit = 1
            while len(values) > 1:
                odd = (level & bit) != 0
                values = [
                    jnp.where(odd, values[i + 1], values[i]) if i + 1 < len(values) else values[i]
                    for i in range(0, len(values), 2)
                ]
                bit = 2 * bit
            V_s[pl.ds(pl.multiple_of(row * 8, 8), 8), :] = values[0]

    def collide(row0, v):
        read = [V_s[pl.ds(row0 * 8 + c, 8, stride=8), :] for c in range(7)]
        u = [read[d] + read[3 + d] for d in range(3)]
        index = read[6].astype(jnp.int32)
        n = [
            jnp.take_along_axis(axis_tab[8 * d : 8 * d + 8, :], index, axis=1) for d in range(3)
        ]
        return rotated(v, u, n)

    def emit(row0, p, v, live):
        new = collide(row0, v)
        for d in range(3):
            offset = p[d] - jnp.floor(p[d]) - 0.5
            vel_out[d, pl.ds(row0, 8), :] = new[d]
            off_out[d, pl.ds(row0, 8), :] = jnp.where(live, offset, 2.0)

    def emit_step(b):
        for i in range(STEP // 8):
            emit(*solvent(b, i))

    def look_loop(b, carry):
        emit_step(jnp.maximum(b - 1, 0))
        look_rows(pl.multiple_of(b * STEP, 8), STEP)
        return carry

    look_rows(SOLV, 2)
    new = collide(SOLV, [bpack[3 + d] for d in range(3)])
    speed = []
    for d in range(3):
        W_s[d] = new[d]
        speed.append(jnp.concatenate([W_s[d, 0:1, :], W_s[d, 1:2, :]], 1))

    def out_copies(part):
        rows = pl.ds(part * HALF, HALF) if part < 2 else pl.ds(RES, SOLV - RES)
        return [
            pltpu.make_async_copy(
                off_out.at[:, rows], off_hbm.at[:, rows], out_sem.at[0, part]
            ),
            pltpu.make_async_copy(
                vel_out.at[:, rows], vel_hbm.at[:, rows], out_sem.at[1, part]
            ),
        ]

    half_kick = 0.5 * step_size / bead_mass

    def substep(t, carry):
        speed, gone, push = carry[0:3], carry[3:6], carry[6:9]
        speed = [speed[d] + half_kick * push[d] for d in range(3)]
        gone = [gone[d] + step_size * speed[d] for d in range(3)]
        place(t + 1, [start[d] + gone[d] for d in range(3)])
        bead_send(t + 1)
        lax.fori_loop(
            HSTEPS * t, jnp.minimum(HSTEPS * (t + 1), STEPS), look_loop, 0
        )

        @pl.when(t == 1)
        def _():
            for copy in out_copies(0):
                copy.start()

        @pl.when(t == 2)
        def _():
            emit_step(STEPS - 1)
            for part in (1, 2):
                for copy in out_copies(part):
                    copy.start()

        bead_arrive(t + 1)
        push = forces(t + 1)
        speed = [speed[d] + half_kick * push[d] for d in range(3)]
        return (*speed, *gone, *push)

    still = jnp.zeros((1, 256), F32)
    last = lax.fori_loop(0, 3, substep, (*speed, still, still, still, *push))
    for d in range(3):
        bpos_out[d] = last[3 + d]
        bvel_out[d] = last[d]
    for part in range(3):
        for copy in out_copies(part):
            copy.wait()

    for g in range(6):
        for copy in mig_copies(g, g ^ 1):
            copy.wait_send()
    for copy in halo:
        copy.wait_send()
    for copy in info:
        copy.wait_send()
    for exchange in range(4):
        for dx, dy, dz in OFFSETS:
            bead_copy(exchange, (dx, dy, dz), slot(-dx, -dy, dz)).wait_send()


def shards(
    sol_pos,
    sol_vel,
    sol_rows,
    mig_pos,
    mig_vel,
    mig_rows,
    bead_pos,
    bead_vel,
    bead_chains,
    bond_list,
    cell_axis,
    shift,
):
    vmem = pl.BlockSpec(memory_space=pltpu.VMEM)
    smem = pl.BlockSpec(memory_space=pltpu.SMEM)
    anywhere = pl.BlockSpec(memory_space=pl.ANY)
    dma = pltpu.SemaphoreType.DMA
    f32 = lambda *shape: pltpu.VMEM(shape, F32)
    bf = lambda *shape: pltpu.VMEM(shape, BF)
    outs = pl.pallas_call(
        kernel,
        out_shape=(
            jax.ShapeDtypeStruct((3, SOLV, 128), F32),
            jax.ShapeDtypeStruct((3, SOLV, 128), F32),
            jax.ShapeDtypeStruct((3, 1, BEADS), F32),
            jax.ShapeDtypeStruct((3, 1, BEADS), F32),
        ),
        in_specs=[smem] * 4 + [anywhere] * 4 + [vmem] * 5,
        out_specs=(anywhere, anywhere, vmem, vmem),
        scratch_shapes=[
            f32(3, SOLV, 128),
            f32(3, SOLV, 128),
            f32(3, SOLV, 128),
            f32(3, SOLV, 128),
            pltpu.VMEM((2, 1, 256), jnp.int32),
            f32(ALL, 128),
            f32(ALL, 128),
            f32(ALL * 8 + 64, 128),
            f32(2 * TROWS + 32, 128),
            bf(256, 128),
            bf(TROWS, 128),
            pltpu.VMEM((72, 128), jnp.int32),
            pltpu.VMEM((6, 1, 128), jnp.int32),
            pltpu.VMEM((6, 1, 128), jnp.int32),
            f32(6, 8, 128),
            f32(4, 40, 256),
            bf(768, 256),
            bf(256, 256),
            f32(8, 256),
            f32(8, 256),
            f32(4, 256),
            f32(4, 256),
            f32(8, 256),
            f32(8, 256),
            f32(4, 256),
            f32(4, 4, 256),
            f32(8, 256),
            f32(8, 256),
            f32(4, 256),
            f32(4, 256),
            f32(8, 256),
            f32(8, 256),
            f32(4, 256),
            f32(4, 4, 256),
            f32(4, 32, 256),
            f32(2 * TROWS, 128),
            bf(TROWS, 256),
            f32(4, 4, 256),
            f32(4, 18, 4, 256),
            f32(128, 256),
            f32(256, 128),
            f32(72, 256),
            f32(32, 256),
            f32(768, 128),
            f32(3, 8, 128),
            dma((3, 6)),
            dma((3, 6)),
            dma((7,)),
            dma((7,)),
            dma((7,)),
            dma((7,)),
            dma((4, 18)),
            dma((4, 18)),
            dma((2, 2)),
            dma((2, 3)),
            pltpu.SemaphoreType.REGULAR((2,)),
        ],
        compiler_params=pltpu.CompilerParams(
            collective_id=0, has_side_effects=True, vmem_limit_bytes=60 * 1024 * 1024
        ),
        name="interval",
    )(
        sol_rows.reshape(1),
        mig_rows.reshape(6),
        bead_chains.reshape(1),
        shift,
        sol_pos.reshape(3, RES, 128),
        sol_vel.reshape(3, RES, 128),
        mig_pos.reshape(3, 6, FACE, 128),
        mig_vel.reshape(3, 6, FACE, 128),
        bead_pos.reshape(3, 1, BEADS),
        bead_vel.reshape(3, 1, BEADS),
        bond_list.reshape(2, 1, BONDS),
        cell_axis.reshape(256, 32),
        jnp.asarray(axis_rows()),
    )
    offset, vel, bpos, bvel = outs
    live = offset < 1.0
    bead_live = jnp.arange(BEADS, dtype=jnp.int32) < CHAIN * bead_chains.reshape(())
    return (
        jnp.where(live, offset + 3.0 * step_size * vel, 0.0).reshape(3, 1, 1, 1, SOLV * 128),
        jnp.where(live, vel, 0.0).reshape(3, 1, 1, 1, SOLV * 128),
        jnp.where(bead_live, bpos, 0.0).reshape(3, 1, 1, 1, BEADS),
        jnp.where(bead_live, bvel, 0.0).reshape(3, 1, 1, 1, BEADS),
    )


def solution(mesh):
    return jax.shard_map(
        shards,
        mesh=mesh,
        in_specs=(
            P(None, "gx", "gy", "gz", None),
            P(None, "gx", "gy", "gz", None),
            P("gx", "gy", "gz"),
            P(None, "gx", "gy", "gz", None, None),
            P(None, "gx", "gy", "gz", None, None),
            P("gx", "gy", "gz", None),
            P(None, "gx", "gy", "gz", None),
            P(None, "gx", "gy", "gz", None),
            P("gx", "gy", "gz"),
            P(None, "gx", "gy", "gz", None),
            P("gx", "gy", "gz"),
            P(),
        ),
        out_specs=(
            P(None, "gx", "gy", "gz", None),
            P(None, "gx", "gy", "gz", None),
            P(None, "gx", "gy", "gz", None),
            P(None, "gx", "gy", "gz", None),
        ),
        check_vma=False,
    )
```
